32 devices in a mesh: grp: 2 (over y), band: 4 (over z), sect: 4 (over x, core).
Axes of the slice: x: 2, y: 2, z: 4, core: 2. Of those that a mesh axis runs over, the one named last changes fastest.
Arguments:
- features: bfloat16 [4, 24, 96, 2048], P('grp', 'band', None, 'sect'), parts along dimension 0, may hold values from -16 to 16
- low_level: bfloat16 [4, 24, 96, 256], P('grp', 'band'), parts along dimension 0, may hold values from -6 to 6
- land_mask: int32 [4, 24], P('grp', 'band'), parts along dimension 0, may hold values from 0 to 1, as said below
- weight_one: bfloat16 [2048, 256], P('sect'), may hold values from -0.125 to 0.125
- weight_dilated: bfloat16 [3, 3, 3, 2048, 256], P(None, None, None, 'sect'), may hold values from -0.046875 to 0.046875
- bias_branch: float32 [4, 256], replicated, may hold values from -3 to 3
- weight_pool: bfloat16 [2048, 256], P('sect'), may hold values from -0.125 to 0.125
- bias_pool: float32 [256], replicated, may hold values from -3 to 3
- weight_project: bfloat16 [1280, 256], replicated, may hold values from -0.15625 to 0.15625
- bias_project: float32 [256], replicated, may hold values from -3 to 3
- weight_reduce: bfloat16 [256, 48], replicated, may hold values from -0.375 to 0.375
- bias_reduce: float32 [48], replicated, may hold values from -3 to 3
- weight_merging: bfloat16 [3, 3, 304, 256], replicated, may hold values from -0.109375 to 0.109375
- bias_merging: float32 [256], replicated, may hold values from -3 to 3
Outputs:
- merged_map: bfloat16 [4, 24, 96, 256], P('grp', 'band'), parts along dimension 0
The draws below stay inside these ranges and needn't reach their ends.
There are 2 independent parts, one for each index of `grp`. The reference program is written for one: setup_inputs(seed, part) draws one part's arguments, and reference() takes and returns one part's arrays. A program takes and returns all parts, laid end to end along the dimension named above; an argument that names none is the same for every part. Nothing has to cross between parts.
Inputs may be any that keep to these rules, and one draw needn't show every extreme that they name: `land_mask`: in every image each aligned block of 6 rows holds at most 4 ones and at least 2 ones, its first and last rows always being ones; in every image some block holds exactly 4.
All inputs are finite; a program needn't handle non-finite values.
Results may differ from the reference program's by a relative error of at most 0.012.
Values may be sent and summed in bfloat16 or wider, within the bound.
A program may use at most 64 MiB of HBM per device.

```python
import jax
import jax.numpy as jnp
from jax import lax

C = 2048
BR = 256
LOW = 256
LOWP = 48
DEC = 256
W = 96
MB = 2
R_DEV = 6
ACT_DEV = 4
H = 24
N_SECT = 4


def draw_features(key, part):
    base = jax.random.fold_in(key, 11)
    key_noise, key_mean, key_rows = jax.random.split(base, 3)
    rough = jax.random.normal(key_noise, (MB, H, W, C), jnp.float32)
    channel_mean = jax.random.normal(key_mean, (C,), jnp.float32) * 0.7
    row_ramp = 1.0 + 2.0 * jnp.arange(H, dtype=jnp.float32) / H
    row_factor = row_ramp[None, :] * jax.random.uniform(key_rows, (MB, H), jnp.float32, 0.5, 1.5)
    values = rough + channel_mean[None, None, None, :] * row_factor[:, :, None, None]
    return jnp.clip(values, -16.0, 16.0).astype(jnp.bfloat16)


def draw_land_mask(key, part):
    base = jax.random.fold_in(key, 7)
    key_count, key_full, key_order = jax.random.split(base, 3)
    band_count = H // R_DEV
    counts = jax.random.randint(key_count, (MB, band_count), ACT_DEV - ACT_DEV // 2, ACT_DEV + 1)
    full_band = jax.random.randint(key_full, (MB, 1), 0, band_count)
    counts = jnp.where(jnp.arange(band_count)[None, :] == full_band, ACT_DEV, counts)
    row_index = jnp.arange(R_DEV, dtype=jnp.int32)
    edge_row = (row_index == 0) | (row_index == R_DEV - 1)
    random_part = (jax.random.randint(key_order, (MB, band_count, R_DEV), 0, 2 ** 20) + 1) * R_DEV + row_index[None, None, :]
    scores = jnp.where(edge_row[None, None, :], row_index[None, None, :], random_part)
    rank_of = jnp.argsort(jnp.argsort(scores, axis=2), axis=2)
    land_rows = (rank_of < counts[:, :, None]).astype(jnp.int32)
    return land_rows.reshape(MB, H)


def shard_levels(key, shape, cuts, smallest, top_value):
    def one(position, parts):
        heights = jax.random.uniform(jax.random.fold_in(jax.random.fold_in(key, 6), position), (parts,), jnp.float32, smallest / len(cuts), top_value / len(cuts))
        return jnp.repeat(jnp.exp(heights), shape[position] // parts).reshape((-1,) + (1,) * (len(shape) - position - 1))

    gain = one(*cuts[0])
    for cut in cuts[1:]:
        gain = gain * one(*cut)
    return gain


def gaussian(own_key, shape, width, limit, cuts=(), held_as=jnp.bfloat16):
    array = width * jax.random.normal(own_key, shape, jnp.float32)
    if cuts:
        array = array * shard_levels(own_key, shape, cuts, -0.22, 0.18)
    return jnp.clip(array, -limit, limit).astype(held_as)


def setup_inputs(seed: int = 0, part: int = 0) -> dict:
    key_list = jax.random.split(jax.random.key(seed), 15)
    part_keys = jax.random.split(jax.random.fold_in(key_list[14], part), 15)
    return {
        "features": draw_features(jax.random.fold_in(jax.random.fold_in(key_list[14], part), 71), part),
        "low_level": gaussian(part_keys[1], (MB, H, W, LOW), 1.0, 6.0, ((1, 4),)),
        "land_mask": draw_land_mask(jax.random.fold_in(jax.random.fold_in(key_list[14], part), 71), part),
        "weight_one": gaussian(key_list[3], (C, BR), C ** -0.5, 0.125, ((0, 4),)),
        "weight_dilated": gaussian(key_list[4], (3, 3, 3, C, BR), (9 * C) ** -0.5, 0.046875, ((3, 4),)),
        "bias_branch": gaussian(key_list[5], (4, BR), 0.5, 3.0, (), jnp.float32),
        "weight_pool": gaussian(key_list[6], (C, BR), C ** -0.5, 0.125, ((0, 4),)),
        "bias_pool": gaussian(key_list[7], (BR,), 0.5, 3.0, (), jnp.float32),
        "weight_project": gaussian(key_list[8], (5 * BR, BR), (5 * BR) ** -0.5, 0.15625),
        "bias_project": gaussian(key_list[9], (BR,), 0.5, 3.0, (), jnp.float32),
        "weight_reduce": gaussian(key_list[10], (LOW, LOWP), LOW ** -0.5, 0.375),
        "bias_reduce": gaussian(key_list[11], (LOWP,), 0.5, 3.0, (), jnp.float32),
        "weight_merging": gaussian(key_list[12], (3, 3, BR + LOWP, DEC), (9 * (BR + LOWP)) ** -0.5, 0.109375),
        "bias_merging": gaussian(key_list[13], (DEC,), 0.5, 3.0, (), jnp.float32),
    }


DILATIONS = (12, 24, 36)
PADDING = 36
PRECISE = lax.Precision.HIGHEST


def group_partial(sample_map, weight_one, weight_dilated, first_channel, group_width):
    height, breadth = sample_map.shape[0], sample_map.shape[1]
    section = sample_map[:, :, first_channel:first_channel + group_width]
    padded = jnp.pad(section, ((PADDING, PADDING), (PADDING, PADDING), (0, 0)))
    partials = [jnp.dot(section.reshape(-1, group_width), weight_one[first_channel:first_channel + group_width], preferred_element_type=jnp.float32)]
    for branch_index, dilation in enumerate(DILATIONS):
        running = jnp.zeros((height * breadth, weight_one.shape[1]), jnp.float32)
        for row_tap in range(3):
            for col_tap in range(3):
                top = PADDING + dilation * (row_tap - 1)
                left = PADDING + dilation * (col_tap - 1)
                tap_rows = padded[top:top + height, left:left + breadth].reshape(-1, group_width)
                running = running + jnp.dot(tap_rows, weight_dilated[branch_index, row_tap, col_tap, first_channel:first_channel + group_width], preferred_element_type=jnp.float32)
        partials.append(running)
    return jnp.concatenate(partials, axis=1).astype(jnp.bfloat16)


def reference(features, low_level, land_mask, weight_one, weight_dilated, bias_branch, weight_pool, bias_pool, weight_project, bias_project, weight_reduce, bias_reduce, weight_merging, bias_merging):
    group_width = C // N_SECT
    results = []
    for sample in range(MB):
        sample_map = features[sample]
        pre_branch = jnp.zeros((H * W, 4 * BR), jnp.float32)
        for group_index in range(N_SECT):
            pre_branch = pre_branch + group_partial(sample_map, weight_one, weight_dilated, group_index * group_width, group_width).astype(jnp.float32)
        branch = jax.nn.relu(pre_branch + bias_branch.reshape(-1)).astype(jnp.bfloat16)
        average = jnp.sum(sample_map, axis=(0, 1), dtype=jnp.float32) / (H * W)
        pooled = jax.nn.relu(jnp.dot(average, weight_pool.astype(jnp.float32), precision=PRECISE) + bias_pool)
        context = jnp.dot(pooled, weight_project[4 * BR:].astype(jnp.float32), precision=PRECISE)
        row_keep = land_mask[sample].astype(jnp.float32)
        projected = jnp.dot(branch, weight_project[:4 * BR], preferred_element_type=jnp.float32) + context + bias_project
        project_out = (jax.nn.relu(projected).reshape(H, W, BR) * row_keep[:, None, None]).astype(jnp.bfloat16)
        low_reduced = jax.nn.relu(jnp.dot(low_level[sample].reshape(-1, LOW), weight_reduce, preferred_element_type=jnp.float32) + bias_reduce).astype(jnp.bfloat16).reshape(H, W, LOWP)
        joined = jnp.concatenate([project_out, low_reduced], axis=2)
        framed = jnp.pad(joined, ((1, 1), (1, 1), (0, 0)))
        running = jnp.zeros((H * W, DEC), jnp.float32)
        for row_tap in range(3):
            for col_tap in range(3):
                running = running + jnp.dot(framed[row_tap:row_tap + H, col_tap:col_tap + W].reshape(-1, BR + LOWP), weight_merging[row_tap, col_tap], preferred_element_type=jnp.float32)
        merged_map = (jax.nn.relu(running + bias_merging).reshape(H, W, DEC) * row_keep[:, None, None]).astype(jnp.bfloat16)
        results.append(merged_map)
    return jnp.stack(results)
```

```python
import functools

import jax
import jax.numpy as jnp
from jax import lax
from jax.experimental import pallas as pl
from jax.experimental.pallas import tpu as pltpu
from jax.sharding import PartitionSpec as P

DILATIONS = (12, 24, 36)
LAND_BLOCK = 6
LAND_MOST = 4
PRECISE = lax.Precision.HIGHEST
MESH = pl.DeviceIdType.MESH
F32 = jnp.float32
BF16 = jnp.bfloat16


def plan(rows, bands):
    off = []
    for k in (1, 2, 3):
        d = DILATIONS[k - 1]
        assert d % rows == 0
        hop = d // rows
        if hop < bands:
            off.append((k, 0, hop))
            off.append((k, 2, hop))
    order = [k for k in (3, 2, 1, 0)]
    return off, order


def kernel(
    dims, mask, feat_h, low_h, w1_h, wd_h, bbr, wpool_h, bpool, wproj_h, bproj, wr, br, wm_h, bm,
    out,
    feat, low, low_halo, w1, wd, wpool, wproj, wm, comp, m_l, m_r,
    part_off, crecv_off, xsend_off, xrecv_off, zsend, zrecv,
    part_own, crecv_own, xsend_own, xrecv_own, keep_off, keep_own,
    sums, pool_s, pool_b, gath, halo, joined, lowred, lowacc, outc,
    loc_sem, lo_s, lo_r, c_s, c_r, x_s, x_r, z_s, z_r, ps_s, ps_r, pb_s, pb_r,
    g_s, g_r, h_s, h_r,
):
    mb, rows, cols, ch, br_w, live, nb, ns, low_w, lowp = dims
    nx = ns // 2
    cs = cols // nx
    off, order = plan(rows, nb)
    n_off = len(off)
    need = [(k, 1) for k in order if k] + [(k, i) for k, i, _ in off]
    pad = (m_l.shape[1] - cols) // 2

    band = lax.axis_index("band")
    sect = lax.axis_index("sect")
    core = lax.rem(sect, 2)
    xi = lax.div(sect, 2)

    locals_ = {}

    def fetch(name, src, dst):
        c = pltpu.make_async_copy(src, dst, loc_sem.at[len(locals_)])
        locals_[name] = c
        c.start()

    fetch("feat", feat_h, feat)
    for k, i, _ in off:
        fetch((k, i), wd_h.at[k - 1, i], wd.at[need.index((k, i))])
    for k in order:
        if k:
            fetch((k, 1), wd_h.at[k - 1, 1], wd.at[need.index((k, 1))])
        else:
            fetch("w1", w1_h, w1)
    fetch("wpool", wpool_h, wpool)
    fetch("low", low_h, low)
    fetch("wproj", wproj_h, wproj)
    fetch("wm", wm_h, wm)

    bar = pltpu.get_barrier_semaphore()
    up_ok = band >= 1
    dn_ok = band + 1 < nb

    def hello(b, s):
        pl.semaphore_signal(bar, inc=1, device_id={"band": b, "sect": s}, device_id_type=MESH)

    for e in range(1, ns):
        hello(band, lax.rem(sect + e, ns))
    for e in range(1, nb):
        hello(lax.rem(band + e, nb), sect)
    for ok, step in ((up_ok, -1), (dn_ok, 1)):
        @pl.when(ok)
        def _(step=step):
            for e in range(1, ns):
                hello(band + step, lax.rem(sect + e, ns))
    sides_held = jnp.minimum(band, 1) + jnp.minimum(nb - 1 - band, 1)
    pl.semaphore_wait(bar, (ns - 1) + (nb - 1) + (ns - 1) * sides_held)

    def rcopy(src, dst, s, r, **where):
        return pltpu.make_async_remote_copy(
            src_ref=src, dst_ref=dst, send_sem=s, recv_sem=r, device_id=where, device_id_type=MESH
        )

    low_up = rcopy(low_h.at[:, 0], low_halo.at[1], lo_s.at[0], lo_r.at[1], band=band - 1, sect=sect)
    low_dn = rcopy(
        low_h.at[:, rows - 1], low_halo.at[0], lo_s.at[1], lo_r.at[0], band=band + 1, sect=sect
    )

    @pl.when(up_ok)
    def _():
        low_up.start()

    @pl.when(dn_ok)
    def _():
        low_dn.start()

    def slots(m):
        on = [mask[m, y] for y in range(rows)]
        slot_of = [jnp.int32(0)] + [None] * (rows - 2) + [jnp.int32(live - 1)]
        row_of = [jnp.int32(0)] * live
        row_of[live - 1] = jnp.int32(rows - 1)
        held = [jnp.int32(0)] * live
        held[0] = on[0]
        held[live - 1] = on[rows - 1]
        count = jnp.int32(0)
        for y in range(1, rows - 1):
            slot_of[y] = jnp.where(on[y] > 0, jnp.minimum(count + 1, live - 1), 0)
            for r in range(1, live - 1):
                hit = jnp.logical_and(on[y] > 0, count == r - 1)
                row_of[r] = jnp.where(hit, y, row_of[r])
                held[r] = jnp.where(hit, 1, held[r])
            count = count + on[y]
        return on, slot_of, row_of, held

    for ref in (m_l, m_r):
        zero = jnp.zeros((ref.shape[0], pad, br_w), F32)
        ref[:, :pad] = zero
        ref[:, pad + cols :] = zero

    locals_["feat"].wait()

    def taps(lhs, n, wref, d):
        mid = jnp.dot(lhs, wref[1], preferred_element_type=F32).reshape(n, cols, br_w)
        m_l[:n, pl.ds(pad, cols)] = jnp.dot(
            lhs, wref[0], preferred_element_type=F32
        ).reshape(n, cols, br_w)
        m_r[:n, pl.ds(pad, cols)] = jnp.dot(
            lhs, wref[2], preferred_element_type=F32
        ).reshape(n, cols, br_w)
        return mid + m_l[:n, pl.ds(pad - d, cols)] + m_r[:n, pl.ds(pad + d, cols)]

    def core_copy(t):
        if t < n_off:
            src, dst = part_off.at[t, 0], crecv_off.at[t]
        else:
            src, dst = part_own.at[t - n_off, 0], crecv_own.at[t - n_off]
        return rcopy(src, dst, c_s.at[t], c_r.at[t], sect=xi * 2 + 1 - core)

    def x_copy(t, e, incoming=False):
        send, recv, u = (
            (xsend_off, xrecv_off, t) if t < n_off else (xsend_own, xrecv_own, t - n_off)
        )
        other = lax.rem(xi + e, nx)
        slot = other if incoming else xi
        return rcopy(
            send.at[u, other], recv.at[u, slot], x_s.at[t, other], x_r.at[t, slot],
            sect=other * 2 + core,
        )

    def first(t):
        def body(step, carry):
            image = jnp.where(step == 0, 1 - core, core)
            if t < n_off:
                k, i, _ = off[t]
                lhs = feat[image].reshape(rows * cols, ch)
                val = taps(lhs, rows, wd.at[need.index((k, i))], DILATIONS[k - 1])
                part_off[t, step] = val.astype(BF16)
            else:
                k = order[t - n_off]
                lhs = comp[image].reshape(live * cols, ch)
                if k:
                    val = taps(lhs, live, wd.at[need.index((k, 1))], DILATIONS[k - 1])
                else:
                    val = jnp.dot(lhs, w1[...], preferred_element_type=F32).reshape(
                        live, cols, br_w
                    )
                part_own[t - n_off, step] = val.astype(BF16)

            @pl.when(step == 0)
            def _():
                core_copy(t).start()
            return carry

        lax.fori_loop(0, 2, body, 0)

    def second(t):
        core_copy(t).wait_recv()
        part, got, send, keep, u = (
            (part_off, crecv_off, xsend_off, keep_off, t)
            if t < n_off
            else (part_own, crecv_own, xsend_own, keep_own, t - n_off)
        )
        for c in range(nx):
            cell = pl.ds(c * cs, cs)
            total = part[u, 1, :, cell].astype(F32) + got[u, :, cell].astype(F32)
            send[u, c] = total.astype(BF16)

            @pl.when(xi == c)
            def _():
                keep[u] = total
        for e in range(1, nx):
            x_copy(t, e).start()

    def shared(t):
        recv, keep, u = (
            (xrecv_off, keep_off, t) if t < n_off else (xrecv_own, keep_own, t - n_off)
        )
        total = keep[u]
        for e in range(1, nx):
            x_copy(t, e, True).wait_recv()
            total = total + recv[u, lax.rem(xi + e, nx)].astype(F32)
        return total

    def sends_to(t):
        k, i, hop = off[t]
        return band + hop < nb if i == 0 else band - hop >= 0

    def gets_from(t):
        k, i, hop = off[t]
        return band - hop >= 0 if i == 0 else band + hop < nb

    def z_copy(t):
        k, i, hop = off[t]
        return rcopy(
            zsend.at[t], zrecv.at[t], z_s.at[t], z_r.at[t],
            band=band + hop if i == 0 else band - hop, sect=sect,
        )

    def third_off(t):
        zsend[t] = shared(t).astype(BF16)
        z_copy(t).start()

    def guarded(fn, t):
        @pl.when(sends_to(t))
        def _():
            fn(t)

    for t in range(n_off):
        locals_[off[t][:2]].wait()
        guarded(first, t)

    facts = [slots(m) for m in range(mb)]
    sums[...] = jnp.zeros_like(sums)
    for m in range(mb):
        for r in range(live):
            comp[m, r] = feat[m, facts[m][2][r]]

    t0 = n_off
    locals_[(order[0], 1) if order[0] else "w1"].wait()
    first(t0)
    for t in range(n_off):
        guarded(second, t)

    locals_["wpool"].wait()
    for m in range(mb):
        acc = jnp.zeros((cols, ch), F32)
        for y in range(rows):
            acc = acc + feat[m, y].astype(F32)
        sums[m : m + 1, :] = jnp.sum(acc, axis=0, keepdims=True)
    pool_s[sect] = jnp.dot(
        sums[...], wpool[...].astype(F32), precision=PRECISE, preferred_element_type=F32
    )

    def pool_sect(e, incoming=False):
        other = lax.rem(sect + e, ns)
        slot = other if incoming else sect
        return rcopy(
            pool_s.at[sect], pool_s.at[slot], ps_s.at[other], ps_r.at[slot], sect=other
        )

    def pool_band(e, incoming=False):
        other = lax.rem(band + e, nb)
        slot = other if incoming else band
        return rcopy(
            pool_b.at[band], pool_b.at[slot], pb_s.at[other], pb_r.at[slot], band=other
        )

    for e in range(1, ns):
        pool_sect(e).start()

    locals_[(order[1], 1) if order[1] else "w1"].wait()
    first(t0 + 1)
    second(t0)
    for t in range(n_off):
        guarded(third_off, t)

    for e in range(1, ns):
        pool_sect(e, True).wait_recv()
    total = pool_s[0]
    for s in range(1, ns):
        total = total + pool_s[s]
    pool_b[band] = total
    for e in range(1, nb):
        pool_band(e).start()

    for u in (2, 3):
        locals_[(order[u], 1) if order[u] else "w1"].wait()
        first(t0 + u)
        second(t0 + u - 1)
    second(t0 + 3)

    locals_["low"].wait()
    locals_["wm"].wait()

    def reduced(v):
        return jax.nn.relu(
            jnp.dot(v, wr[...], preferred_element_type=F32) + br[...]
        ).astype(BF16)

    for m in range(mb):
        lowred[m, 1 : rows + 1] = reduced(low[m].reshape(rows * cols, low_w)).reshape(
            rows, cols, lowp
        )
    for side, at, ok, copy in ((0, 0, up_ok, low_dn), (1, rows + 1, dn_ok, low_up)):
        @pl.when(ok)
        def _(side=side, at=at, copy=copy):
            copy.wait_recv()
            for m in range(mb):
                lowred[m, at] = reduced(low_halo[side, m])

        @pl.when(jnp.logical_not(ok))
        def _(at=at):
            for m in range(mb):
                lowred[m, at] = jnp.zeros((cols, lowp), BF16)

    def merged(source, m, lo, n):
        row_of = facts[m][2]
        sides = [None] * 3
        for i in range(3):
            lhs = jnp.concatenate([source[m, row_of[r] + i] for r in range(live)], axis=0)
            for j in range(3):
                term = jnp.dot(
                    lhs, wm[i, j, lo : lo + n], preferred_element_type=F32
                )
                sides[j] = term if sides[j] is None else sides[j] + term
        m_l[:live, pl.ds(pad, cols)] = sides[0].reshape(live, cols, br_w)
        m_r[:live, pl.ds(pad, cols)] = sides[2].reshape(live, cols, br_w)
        return (
            sides[1].reshape(live, cols, br_w)
            + m_l[:live, pl.ds(pad - 1, cols)]
            + m_r[:live, pl.ds(pad + 1, cols)]
        )

    for m in range(mb):
        lowacc[m] = merged(lowred, m, br_w, lowp) + bm[...].reshape(1, 1, br_w)

    locals_["wproj"].wait()
    for e in range(1, nb):
        pool_band(e, True).wait_recv()
    total = pool_b[0]
    for b in range(1, nb):
        total = total + pool_b[b]
    pooled = jax.nn.relu(total / (nb * rows * cols) + bpool[...])
    context = jnp.dot(
        pooled, wproj[4 * br_w :].astype(F32), precision=PRECISE, preferred_element_type=F32
    )
    mine = context[0:1]
    for m in range(1, mb):
        mine = jnp.where(core == m, context[m : m + 1], mine)
    base = mine + bproj[...]

    _, _, own_row, own_held = slots(core)
    acc = jnp.zeros((live * cs, br_w), F32)
    for u, k in enumerate(order):
        keep_own[u] = shared(t0 + u)
        for t in range(n_off):
            if off[t][0] == k:
                @pl.when(gets_from(t))
                def _(t=t, u=u):
                    z_copy(t).wait_recv()
                    for r in range(live):
                        keep_own[u, r] = keep_own[u, r] + zrecv[t, own_row[r]].astype(F32)
        branch = jax.nn.relu(keep_own[u] + bbr[k : k + 1].reshape(1, 1, br_w)).astype(BF16)
        acc = acc + jnp.dot(
            branch.reshape(live * cs, br_w), wproj[k * br_w : (k + 1) * br_w],
            preferred_element_type=F32,
        )
    done = jax.nn.relu(acc + base).reshape(live, cs, br_w)
    for r in range(live):
        gath[sect, r] = (done[r] * own_held[r].astype(F32)).astype(BF16)

    def gather_copy(e, incoming=False):
        other = lax.rem(sect + e, ns)
        slot = other if incoming else sect
        return rcopy(gath.at[sect], gath.at[slot], g_s.at[other], g_r.at[slot], sect=other)

    def halo_copy(side, e, incoming=False):
        other = lax.rem(sect + e, ns)
        slot = other if incoming else sect
        src = gath.at[sect, live - 1 if side == 0 else 0]
        return rcopy(
            src, halo.at[side, slot], h_s.at[side, other], h_r.at[side, slot],
            band=band + 1 if side == 0 else band - 1, sect=other,
        )

    for e in range(1, ns):
        gather_copy(e).start()
    for side, ok in ((0, dn_ok), (1, up_ok)):
        @pl.when(ok)
        def _(side=side):
            for e in range(ns):
                halo_copy(side, e).start()
    for e in range(1, ns):
        gather_copy(e, True).wait_recv()
    for m in range(mb):
        on, slot_of, _, _ = facts[m]
        for y in range(rows):
            for c in range(nx):
                joined[m, y + 1, pl.ds(c * cs, cs)] = (
                    gath[c * 2 + m, slot_of[y]].astype(F32) * on[y].astype(F32)
                ).astype(BF16)
    for side, at, ok in ((0, 0, up_ok), (1, rows + 1, dn_ok)):
        @pl.when(ok)
        def _(side=side, at=at):
            for e in range(ns):
                halo_copy(side, e, True).wait_recv()
            for m in range(mb):
                for c in range(nx):
                    joined[m, at, pl.ds(c * cs, cs)] = halo[side, c * 2 + m]

        @pl.when(jnp.logical_not(ok))
        def _(at=at):
            for m in range(mb):
                joined[m, at] = jnp.zeros((cols, br_w), BF16)

    for m in range(mb):
        on, slot_of, _, _ = facts[m]
        outc[...] = jax.nn.relu(merged(joined, m, 0, br_w) + lowacc[m])
        for y in range(rows):
            out[m, y] = (outc[slot_of[y]] * on[y].astype(F32)).astype(BF16)

    @pl.when(up_ok)
    def _():
        low_up.wait_send()

    @pl.when(dn_ok)
    def _():
        low_dn.wait_send()

    def left(t):
        core_copy(t).wait_send()
        for e in range(1, nx):
            x_copy(t, e).wait_send()

    for t in range(n_off):
        guarded(left, t)
        guarded(lambda t: z_copy(t).wait_send(), t)
    for u in range(4):
        left(t0 + u)
    for e in range(1, ns):
        pool_sect(e).wait_send()
        gather_copy(e).wait_send()
    for e in range(1, nb):
        pool_band(e).wait_send()
    for side, ok in ((0, dn_ok), (1, up_ok)):
        @pl.when(ok)
        def _(side=side):
            for e in range(ns):
                halo_copy(side, e).wait_send()


def shards(
    features, low_level, land_mask, weight_one, weight_dilated, bias_branch, weight_pool,
    bias_pool, weight_project, bias_project, weight_reduce, bias_reduce, weight_merging,
    bias_merging,
):
    mb, rows, cols, ch = features.shape
    br_w = weight_project.shape[1]
    low_w, lowp = weight_reduce.shape
    nb, ns = lax.axis_size("band"), lax.axis_size("sect")
    nx = ns // 2
    cs = cols // nx
    assert mb == 2 and ns % 2 == 0
    live = rows // LAND_BLOCK * LAND_MOST if rows % LAND_BLOCK == 0 else rows
    off, order = plan(rows, nb)
    n_off = max(len(off), 1)
    n_all = len(off) + 4
    pad = -(-max(DILATIONS) // 8) * 8
    vm, dma = pltpu.VMEM, pltpu.SemaphoreType.DMA
    dims = (mb, rows, cols, ch, br_w, live, nb, ns, low_w, lowp)
    scratch = [
        vm(features.shape, BF16),
        vm(low_level.shape, BF16),
        vm((2, mb, cols, low_w), BF16),
        vm(weight_one.shape, BF16),
        vm((3 + len(off), 3, ch, br_w), BF16),
        vm(weight_pool.shape, BF16),
        vm(weight_project.shape, BF16),
        vm(weight_merging.shape, BF16),
        vm((mb, live, cols, ch), BF16),
        vm((rows, cols + 2 * pad, br_w), F32),
        vm((rows, cols + 2 * pad, br_w), F32),
        vm((n_off, 2, rows, cols, br_w), BF16),
        vm((n_off, rows, cols, br_w), BF16),
        vm((n_off, nx, rows, cs, br_w), BF16),
        vm((n_off, nx, rows, cs, br_w), BF16),
        vm((n_off, rows, cs, br_w), BF16),
        vm((n_off, rows, cs, br_w), BF16),
        vm((4, 2, live, cols, br_w), BF16),
        vm((4, live, cols, br_w), BF16),
        vm((4, nx, live, cs, br_w), BF16),
        vm((4, nx, live, cs, br_w), BF16),
        vm((n_off, rows, cs, br_w), F32),
        vm((4, live, cs, br_w), F32),
        vm((8, ch), F32),
        vm((ns, 8, br_w), F32),
        vm((nb, 8, br_w), F32),
        vm((ns, live, cs, br_w), BF16),
        vm((2, ns, cs, br_w), BF16),
        vm((mb, rows + 2, cols, br_w), BF16),
        vm((mb, rows + 2, cols, lowp), BF16),
        vm((mb, live, cols, br_w), F32),
        vm((live, cols, br_w), F32),
        dma((10 + len(off),)),
        dma((2,)),
        dma((2,)),
        dma((n_all,)),
        dma((n_all,)),
        dma((n_all, nx)),
        dma((n_all, nx)),
        dma((n_off,)),
        dma((n_off,)),
        dma((ns,)),
        dma((ns,)),
        dma((nb,)),
        dma((nb,)),
        dma((ns,)),
        dma((ns,)),
        dma((2, ns)),
        dma((2, ns)),
    ]
    anym = pl.BlockSpec(memory_space=pl.ANY)
    vmem = pl.BlockSpec(memory_space=pltpu.VMEM)
    smem = pl.BlockSpec(memory_space=pltpu.SMEM)
    return pl.pallas_call(
        functools.partial(kernel, dims),
        out_shape=jax.ShapeDtypeStruct((mb, rows, cols, weight_merging.shape[3]), BF16),
        in_specs=[
            smem, anym, anym, anym, anym, vmem, anym, vmem, anym, vmem, vmem, vmem, anym, vmem,
        ],
        out_specs=vmem,
        scratch_shapes=scratch,
        compiler_params=pltpu.CompilerParams(
            collective_id=0, has_side_effects=True, vmem_limit_bytes=60 * 1024 * 1024
        ),
    )(
        land_mask, features, low_level, weight_one, weight_dilated, bias_branch, weight_pool,
        bias_pool.reshape(1, -1), weight_project, bias_project.reshape(1, -1), weight_reduce,
        bias_reduce.reshape(1, -1), weight_merging, bias_merging.reshape(1, -1),
    )


def solution(mesh):
    in_specs = (
        P("grp", "band", None, "sect"),
        P("grp", "band", None, None),
        P("grp", "band"),
        P("sect", None),
        P(None, None, None, "sect", None),
        P(),
        P("sect", None),
        P(),
        P(),
        P(),
        P(),
        P(),
        P(),
        P(),
    )
    out_specs = P("grp", "band", None, None)
    return jax.shard_map(shards, mesh=mesh, in_specs=in_specs, out_specs=out_specs, check_vma=False)
```

```python
import functools

import jax
import jax.numpy as jnp
from jax import lax
from jax.experimental import pallas as pl
from jax.experimental.pallas import tpu as pltpu
from jax.sharding import PartitionSpec as P

DILATIONS = (12, 24, 36)
LAND_BLOCK = 6
LAND_MOST = 4
PRECISE = lax.Precision.HIGHEST
MESH = pl.DeviceIdType.MESH
F32 = jnp.float32
BF16 = jnp.bfloat16


def plan(rows, bands):
    off = []
    for k in (1, 2, 3):
        d = DILATIONS[k - 1]
        assert d % rows == 0
        hop = d // rows
        if hop < bands:
            off.append((k, 0, hop))
            off.append((k, 2, hop))
    order = [3, 2, 0, 1]
    return off, order


def kernel(
    dims, mask, feat_h, low_h, w1_h, wd_h, bbr, wpool_h, bpool, wproj_h, bproj, wr, br, wm_h, bm,
    out,
    feat, low, low_halo, w1, wd, wpool, wproj, wmp, wml, comp, m_l, m_r,
    part_off, crecv_off, xsend_off, xrecv_off, zsend, zrecv,
    part_own, crecv_own, xsend_own, xrecv_own, keep_off, keep_own,
    sums, pool_s, pool_b, gath, gath_b, halo, joined, lowred, lowacc, outc,
    loc_sem, lo_s, lo_r, c_s, c_r, x_s, x_r, z_s, z_r, ps_s, ps_r, pb_s, pb_r,
    gx_s, gx_r, gc_s, gc_r, hx_s, hx_r, hc_s, hc_r,
):
    mb, rows, cols, ch, br_w, live, nb, ns, low_w, lowp = dims
    nx = ns // 2
    cs = cols // nx
    off, order = plan(rows, nb)
    n_off = len(off)
    need = [(k, 1) for k in order if k] + [(k, i) for k, i, _ in off]
    pad = (m_l.shape[1] - cols) // 2

    band = lax.axis_index("band")
    sect = lax.axis_index("sect")
    core = lax.rem(sect, 2)
    xi = lax.div(sect, 2)

    locals_ = {}

    def fetch(name, src, dst):
        c = pltpu.make_async_copy(src, dst, loc_sem.at[len(locals_)])
        locals_[name] = c
        c.start()

    fetch("feat", feat_h, feat)
    for k, i, _ in off:
        fetch((k, i), wd_h.at[k - 1, i], wd.at[need.index((k, i))])
    for k in order:
        if k:
            fetch((k, 1), wd_h.at[k - 1, 1], wd.at[need.index((k, 1))])
        else:
            fetch("w1", w1_h, w1)
    fetch("wpool", wpool_h, wpool)
    fetch("low", low_h, low)
    fetch("wproj", wproj_h, wproj)
    fetch("wml", wm_h.at[:, :, pl.ds(br_w, lowp)], wml)
    for i in range(3):
        for j in range(3):
            fetch(("wmp", i, j), wm_h.at[i, j, pl.ds(0, br_w)], wmp.at[j, pl.ds(i * br_w, br_w)])

    bar = pltpu.get_barrier_semaphore()
    up_ok = band >= 1
    dn_ok = band + 1 < nb

    def hello(b, s):
        pl.semaphore_signal(bar, inc=1, device_id={"band": b, "sect": s}, device_id_type=MESH)

    for e in range(1, ns):
        hello(band, lax.rem(sect + e, ns))
    for e in range(1, nb):
        hello(lax.rem(band + e, nb), sect)
    for ok, step in ((up_ok, -1), (dn_ok, 1)):
        @pl.when(ok)
        def _(step=step):
            for e in range(1, nx):
                hello(band + step, lax.rem(sect + 2 * e, ns))
    def rcopy(src, dst, s, r, **where):
        return pltpu.make_async_remote_copy(
            src_ref=src, dst_ref=dst, send_sem=s, recv_sem=r, device_id=where, device_id_type=MESH
        )

    low_up = rcopy(low_h.at[:, 0], low_halo.at[1], lo_s.at[0], lo_r.at[1], band=band - 1, sect=sect)
    low_dn = rcopy(
        low_h.at[:, rows - 1], low_halo.at[0], lo_s.at[1], lo_r.at[0], band=band + 1, sect=sect
    )

    def slots(m):
        on = [mask[m, y] for y in range(rows)]
        slot_of = [jnp.int32(0)] + [None] * (rows - 2) + [jnp.int32(live - 1)]
        row_of = [jnp.int32(0)] * live
        row_of[live - 1] = jnp.int32(rows - 1)
        held = [jnp.int32(0)] * live
        held[0] = on[0]
        held[live - 1] = on[rows - 1]
        count = jnp.int32(0)
        for y in range(1, rows - 1):
            slot_of[y] = jnp.where(on[y] > 0, jnp.minimum(count + 1, live - 1), 0)
            for r in range(1, live - 1):
                hit = jnp.logical_and(on[y] > 0, count == r - 1)
                row_of[r] = jnp.where(hit, y, row_of[r])
                held[r] = jnp.where(hit, 1, held[r])
            count = count + on[y]
        return on, slot_of, row_of, held

    for ref in (m_l, m_r):
        zero = jnp.zeros((ref.shape[0], pad, br_w), F32)
        ref[:, :pad] = zero
        ref[:, pad + cols :] = zero
    for at in (0, rows + 1):
        joined[:, at] = jnp.zeros((mb, cols, br_w), BF16)

    locals_["feat"].wait()

    def taps(lhs, n, wref, d):
        mid = jnp.dot(lhs, wref[1], preferred_element_type=F32).reshape(n, cols, br_w)
        m_l[:n, pl.ds(pad, cols)] = jnp.dot(
            lhs, wref[0], preferred_element_type=F32
        ).reshape(n, cols, br_w)
        m_r[:n, pl.ds(pad, cols)] = jnp.dot(
            lhs, wref[2], preferred_element_type=F32
        ).reshape(n, cols, br_w)
        return mid + m_l[:n, pl.ds(pad - d, cols)] + m_r[:n, pl.ds(pad + d, cols)]

    def core_copy(t):
        if t < n_off:
            src, dst = part_off.at[t, 0], crecv_off.at[t]
        else:
            src, dst = part_own.at[t - n_off, 0], crecv_own.at[t - n_off]
        return rcopy(src, dst, c_s.at[t], c_r.at[t], sect=xi * 2 + 1 - core)

    def x_copy(t, e, incoming=False):
        send, recv, u = (
            (xsend_off, xrecv_off, t) if t < n_off else (xsend_own, xrecv_own, t - n_off)
        )
        other = lax.rem(xi + e, nx)
        slot = other if incoming else xi
        return rcopy(
            send.at[u, other], recv.at[u, slot], x_s.at[t, other], x_r.at[t, slot],
            sect=other * 2 + core,
        )

    def first(t):
        def body(step, carry):
            image = jnp.where(step == 0, 1 - core, core)
            if t < n_off:
                k, i, _ = off[t]
                lhs = feat[image].reshape(rows * cols, ch)
                val = taps(lhs, rows, wd.at[need.index((k, i))], DILATIONS[k - 1])
                part_off[t, step] = val.astype(BF16)
            else:
                k = order[t - n_off]
                lhs = comp[image].reshape(live * cols, ch)
                if k:
                    val = taps(lhs, live, wd.at[need.index((k, 1))], DILATIONS[k - 1])
                else:
                    val = jnp.dot(lhs, w1[...], preferred_element_type=F32).reshape(
                        live, cols, br_w
                    )
                part_own[t - n_off, step] = val.astype(BF16)

            if t >= n_off:
                @pl.when(step == 0)
                def _():
                    core_copy(t).start()
            return carry

        lax.fori_loop(0, 2, body, 0)

    def second(t):
        core_copy(t).wait_recv()
        part, got, send, keep, u = (
            (part_off, crecv_off, xsend_off, keep_off, t)
            if t < n_off
            else (part_own, crecv_own, xsend_own, keep_own, t - n_off)
        )
        for c in range(nx):
            cell = pl.ds(c * cs, cs)
            total = part[u, 1, :, cell].astype(F32) + got[u, :, cell].astype(F32)
            send[u, c] = total.astype(BF16)

            @pl.when(xi == c)
            def _():
                keep[u] = total
        for e in range(1, nx):
            x_copy(t, e).start()

    def shared(t):
        recv, keep, u = (
            (xrecv_off, keep_off, t) if t < n_off else (xrecv_own, keep_own, t - n_off)
        )
        total = keep[u]
        for e in range(1, nx):
            x_copy(t, e, True).wait_recv()
            total = total + recv[u, lax.rem(xi + e, nx)].astype(F32)
        return total

    def sends_to(t):
        k, i, hop = off[t]
        return band + hop < nb if i == 0 else band - hop >= 0

    def gets_from(t):
        k, i, hop = off[t]
        return band - hop >= 0 if i == 0 else band + hop < nb

    def z_copy(t):
        k, i, hop = off[t]
        return rcopy(
            zsend.at[t], zrecv.at[t], z_s.at[t], z_r.at[t],
            band=band + hop if i == 0 else band - hop, sect=sect,
        )

    def third_off(t):
        zsend[t] = shared(t).astype(BF16)
        z_copy(t).start()

    def guarded(fn, t):
        @pl.when(sends_to(t))
        def _():
            fn(t)

    for t in range(n_off):
        locals_[off[t][:2]].wait()
        guarded(first, t)

    sides_held = jnp.minimum(band, 1) + jnp.minimum(nb - 1 - band, 1)
    pl.semaphore_wait(bar, (ns - 1) + (nb - 1) + (nx - 1) * sides_held)

    for t in range(n_off):
        guarded(lambda t: core_copy(t).start(), t)
    @pl.when(up_ok)
    def _():
        low_up.start()

    @pl.when(dn_ok)
    def _():
        low_dn.start()

    facts = [slots(m) for m in range(mb)]
    sums[...] = jnp.zeros_like(sums)
    for m in range(mb):
        for r in range(live):
            comp[m, r] = feat[m, facts[m][2][r]]

    t0 = n_off
    locals_[(order[0], 1) if order[0] else "w1"].wait()
    first(t0)
    for t in range(n_off):
        guarded(second, t)

    locals_["wpool"].wait()
    for m in range(mb):
        acc = jnp.zeros((cols, ch), F32)
        for y in range(rows):
            acc = acc + feat[m, y].astype(F32)
        sums[m : m + 1, :] = jnp.sum(acc, axis=0, keepdims=True)
    pool_s[sect] = jnp.dot(
        sums[...], wpool[...].astype(F32), precision=PRECISE, preferred_element_type=F32
    )

    def pool_sect(e, incoming=False):
        other = lax.rem(sect + e, ns)
        slot = other if incoming else sect
        return rcopy(
            pool_s.at[sect], pool_s.at[slot], ps_s.at[other], ps_r.at[slot], sect=other
        )

    def pool_band(e, incoming=False):
        other = lax.rem(band + e, nb)
        slot = other if incoming else band
        return rcopy(
            pool_b.at[band], pool_b.at[slot], pb_s.at[other], pb_r.at[slot], band=other
        )

    for e in range(1, ns):
        pool_sect(e).start()

    locals_[(order[1], 1) if order[1] else "w1"].wait()
    first(t0 + 1)
    second(t0)
    for t in range(n_off):
        guarded(third_off, t)

    for e in range(1, ns):
        pool_sect(e, True).wait_recv()
    total = pool_s[0]
    for s in range(1, ns):
        total = total + pool_s[s]
    pool_b[band] = total
    for e in range(1, nb):
        pool_band(e).start()

    for u in (2, 3):
        locals_[(order[u], 1) if order[u] else "w1"].wait()
        first(t0 + u)
        second(t0 + u - 1)
    second(t0 + 3)

    locals_["low"].wait()
    locals_["wml"].wait()

    def reduced(v):
        return jax.nn.relu(
            lax.dot_general(
                v, wr[...], (((1,), (1,)), ((), ())), preferred_element_type=F32
            )
            + br[...]
        ).astype(BF16)

    for m in range(mb):
        lowred[m, 1 : rows + 1] = reduced(low[m].reshape(rows * cols, low_w)).reshape(
            rows, cols, lowp
        )
    for side, at, ok, copy in ((0, 0, up_ok, low_dn), (1, rows + 1, dn_ok, low_up)):
        @pl.when(ok)
        def _(side=side, at=at, copy=copy):
            copy.wait_recv()
            for m in range(mb):
                lowred[m, at] = reduced(low_halo[side, m])

        @pl.when(jnp.logical_not(ok))
        def _(at=at):
            for m in range(mb):
                lowred[m, at] = jnp.zeros((cols, lowp), BF16)

    def stash(terms):
        for ref, term in zip((m_l, m_r), (terms[0], terms[2])):
            ref[:live, pl.ds(pad, cols)] = term.reshape(live, cols, br_w)
        outc[...] = terms[1].reshape(live, cols, br_w)

    def combined():
        return outc[...] + m_l[:live, pl.ds(pad - 1, cols)] + m_r[:live, pl.ds(pad + 1, cols)]

    for m in range(mb):
        row_of = facts[m][2]
        terms = [None] * 3
        for i in range(3):
            lhs = jnp.concatenate([lowred[m, row_of[r] + i] for r in range(live)], axis=0)
            for j in range(3):
                term = jnp.dot(lhs, wml[i, j], preferred_element_type=F32)
                terms[j] = term if i == 0 else terms[j] + term
        stash(terms)
        lowacc[m] = combined() + bm[...].reshape(1, 1, br_w)

    locals_["wproj"].wait()
    for e in range(1, nb):
        pool_band(e, True).wait_recv()
    total = pool_b[0]
    for b in range(1, nb):
        total = total + pool_b[b]
    pooled = jax.nn.relu(total / (nb * rows * cols) + bpool[...])
    context = jnp.dot(
        pooled, wproj[4 * br_w :].astype(F32), precision=PRECISE, preferred_element_type=F32
    )
    mine = context[0:1]
    for m in range(1, mb):
        mine = jnp.where(core == m, context[m : m + 1], mine)
    base = mine + bproj[...]

    _, _, own_row, own_held = slots(core)
    acc = jnp.zeros((live * cs, br_w), F32)
    for u, k in enumerate(order):
        keep_own[u] = shared(t0 + u)
        for t in range(n_off):
            if off[t][0] == k:
                @pl.when(gets_from(t))
                def _(t=t, u=u):
                    z_copy(t).wait_recv()
                    for r in range(live):
                        keep_own[u, r] = keep_own[u, r] + zrecv[t, own_row[r]].astype(F32)
        branch = jax.nn.relu(keep_own[u] + bbr[k : k + 1].reshape(1, 1, br_w)).astype(BF16)
        acc = acc + jnp.dot(
            branch.reshape(live * cs, br_w), wproj[k * br_w : (k + 1) * br_w],
            preferred_element_type=F32,
        )
    done = jax.nn.relu(acc + base).reshape(live, cs, br_w)
    for r in range(live):
        gath[xi, r] = (done[r] * own_held[r].astype(F32)).astype(BF16)

    peer = xi * 2 + 1 - core

    def gather_x(e, incoming=False):
        other = lax.rem(xi + e, nx)
        slot = other if incoming else xi
        return rcopy(
            gath.at[xi], gath.at[slot], gx_s.at[other], gx_r.at[slot], sect=other * 2 + core
        )

    def gather_core(c):
        return rcopy(gath.at[c], gath_b.at[c], gc_s.at[c], gc_r.at[c], sect=peer)

    def halo_x(side, e, incoming=False):
        other = lax.rem(xi + e, nx)
        slot = other if incoming else xi
        src = gath.at[xi, live - 1 if side == 0 else 0]
        return rcopy(
            src, halo.at[side, slot * 2 + core], hx_s.at[side, other], hx_r.at[side, slot],
            band=band + 1 if side == 0 else band - 1, sect=other * 2 + core,
        )

    def halo_core(side, c, incoming=False):
        cell = c * 2 + (1 - core if incoming else core)
        return rcopy(
            halo.at[side, cell], halo.at[side, cell], hc_s.at[side, c], hc_r.at[side, c], sect=peer
        )

    for e in range(1, nx):
        gather_x(e).start()
    for side, ok in ((0, dn_ok), (1, up_ok)):
        @pl.when(ok)
        def _(side=side):
            for e in range(nx):
                halo_x(side, e).start()
    gather_core(xi).start()
    for i in range(3):
        for j in range(3):
            locals_[("wmp", i, j)].wait()
    for e in range(1, nx):
        gather_x(e, True).wait_recv()
        gather_core(lax.rem(xi + e, nx)).start()

    for step in range(2):
        image = core if step == 0 else 1 - core
        on, slot_of, row_of, _ = slots(image)
        cells = gath if step == 0 else gath_b
        if step == 1:
            for c in range(nx):
                gather_core(c).wait_recv()
        for y in range(rows):
            for c in range(nx):
                joined[image, y + 1, pl.ds(c * cs, cs)] = (
                    cells[c, slot_of[y]].astype(F32) * on[y].astype(F32)
                ).astype(BF16)
        lhs = jnp.concatenate(
            [
                jnp.concatenate([joined[image, row_of[r] + i] for r in range(live)], axis=0)
                for i in range(3)
            ],
            axis=1,
        )
        stash([jnp.dot(lhs, wmp[j], preferred_element_type=F32) for j in range(3)])
        for side, ok in ((0, up_ok), (1, dn_ok)):
            @pl.when(ok)
            def _(side=side, step=step, image=image):
                for e in range(nx):
                    if step == 0:
                        halo_x(side, e, True).wait_recv()
                        halo_core(side, lax.rem(xi + e, nx)).start()
                    else:
                        halo_core(side, e, True).wait_recv()
                edge = jnp.concatenate([halo[side, c * 2 + image] for c in range(nx)], axis=0)
                at = 0 if side == 0 else live - 1
                tap = pl.ds(2 * br_w * side, br_w)
                add = [
                    jnp.dot(edge, wmp[j, tap], preferred_element_type=F32) for j in range(3)
                ]
                m_l[at, pl.ds(pad, cols)] = m_l[at, pl.ds(pad, cols)] + add[0]
                outc[at] = outc[at] + add[1]
                m_r[at, pl.ds(pad, cols)] = m_r[at, pl.ds(pad, cols)] + add[2]
        outc[...] = jax.nn.relu(combined() + lowacc[image])
        for y in range(rows):
            out[image, y] = outc[slot_of[y]].astype(BF16)

    @pl.when(up_ok)
    def _():
        low_up.wait_send()

    @pl.when(dn_ok)
    def _():
        low_dn.wait_send()

    def left(t):
        core_copy(t).wait_send()
        for e in range(1, nx):
            x_copy(t, e).wait_send()

    for t in range(n_off):
        guarded(left, t)
        guarded(lambda t: z_copy(t).wait_send(), t)
    for u in range(4):
        left(t0 + u)
    for e in range(1, ns):
        pool_sect(e).wait_send()
    for e in range(1, nb):
        pool_band(e).wait_send()
    for e in range(1, nx):
        gather_x(e).wait_send()
    for c in range(nx):
        gather_core(c).wait_send()
    for side, ok in ((0, dn_ok), (1, up_ok)):
        @pl.when(ok)
        def _(side=side):
            for e in range(nx):
                halo_x(side, e).wait_send()
    for side, ok in ((0, up_ok), (1, dn_ok)):
        @pl.when(ok)
        def _(side=side):
            for c in range(nx):
                halo_core(side, c).wait_send()


def shards(
    features, low_level, land_mask, weight_one, weight_dilated, bias_branch, weight_pool,
    bias_pool, weight_project, bias_project, weight_reduce, bias_reduce, weight_merging,
    bias_merging,
):
    mb, rows, cols, ch = features.shape
    br_w = weight_project.shape[1]
    low_w, lowp = weight_reduce.shape
    nb, ns = lax.axis_size("band"), lax.axis_size("sect")
    nx = ns // 2
    cs = cols // nx
    assert mb == 2 and ns % 2 == 0
    live = rows // LAND_BLOCK * LAND_MOST if rows % LAND_BLOCK == 0 else rows
    off, order = plan(rows, nb)
    n_off = max(len(off), 1)
    n_all = len(off) + 4
    pad = -(-max(DILATIONS) // 8) * 8
    vm, dma = pltpu.VMEM, pltpu.SemaphoreType.DMA
    dims = (mb, rows, cols, ch, br_w, live, nb, ns, low_w, lowp)
    scratch = [
        vm(features.shape, BF16),
        vm(low_level.shape, BF16),
        vm((2, mb, cols, low_w), BF16),
        vm(weight_one.shape, BF16),
        vm((3 + len(off), 3, ch, br_w), BF16),
        vm(weight_pool.shape, BF16),
        vm(weight_project.shape, BF16),
        vm((3, 3 * br_w, weight_merging.shape[3]), BF16),
        vm((3, 3, lowp, weight_merging.shape[3]), BF16),
        vm((mb, live, cols, ch), BF16),
        vm((rows, cols + 2 * pad, br_w), F32),
        vm((rows, cols + 2 * pad, br_w), F32),
        vm((n_off, 2, rows, cols, br_w), BF16),
        vm((n_off, rows, cols, br_w), BF16),
        vm((n_off, nx, rows, cs, br_w), BF16),
        vm((n_off, nx, rows, cs, br_w), BF16),
        vm((n_off, rows, cs, br_w), BF16),
        vm((n_off, rows, cs, br_w), BF16),
        vm((4, 2, live, cols, br_w), BF16),
        vm((4, live, cols, br_w), BF16),
        vm((4, nx, live, cs, br_w), BF16),
        vm((4, nx, live, cs, br_w), BF16),
        vm((n_off, rows, cs, br_w), F32),
        vm((4, live, cs, br_w), F32),
        vm((8, ch), F32),
        vm((ns, 8, br_w), F32),
        vm((nb, 8, br_w), F32),
        vm((nx, live, cs, br_w), BF16),
        vm((nx, live, cs, br_w), BF16),
        vm((2, ns, cs, br_w), BF16),
        vm((mb, rows + 2, cols, br_w), BF16),
        vm((mb, rows + 2, cols, lowp), BF16),
        vm((mb, live, cols, br_w), F32),
        vm((live, cols, br_w), F32),
        dma((19 + len(off),)),
        dma((2,)),
        dma((2,)),
        dma((n_all,)),
        dma((n_all,)),
        dma((n_all, nx)),
        dma((n_all, nx)),
        dma((n_off,)),
        dma((n_off,)),
        dma((ns,)),
        dma((ns,)),
        dma((nb,)),
        dma((nb,)),
        dma((nx,)),
        dma((nx,)),
        dma((nx,)),
        dma((nx,)),
        dma((2, nx)),
        dma((2, nx)),
        dma((2, nx)),
        dma((2, nx)),
    ]
    anym = pl.BlockSpec(memory_space=pl.ANY)
    vmem = pl.BlockSpec(memory_space=pltpu.VMEM)
    smem = pl.BlockSpec(memory_space=pltpu.SMEM)
    merged_map = pl.pallas_call(
        functools.partial(kernel, dims),
        out_shape=jax.ShapeDtypeStruct((mb, rows, cols, weight_merging.shape[3]), BF16),
        in_specs=[
            smem, anym, anym, anym, anym, vmem, anym, vmem, anym, vmem, vmem, vmem, anym, vmem,
        ],
        out_specs=vmem,
        scratch_shapes=scratch,
        compiler_params=pltpu.CompilerParams(
            collective_id=0, has_side_effects=True, vmem_limit_bytes=60 * 1024 * 1024
        ),
    )(
        land_mask, features, low_level, weight_one, weight_dilated, bias_branch, weight_pool,
        bias_pool.reshape(1, -1), weight_project, bias_project.reshape(1, -1), weight_reduce.T,
        bias_reduce.reshape(1, -1), weight_merging, bias_merging.reshape(1, -1),
    )
    return jnp.where(land_mask[:, :, None, None] != 0, merged_map, jnp.zeros_like(merged_map))


def solution(mesh):
    in_specs = (
        P("grp", "band", None, "sect"),
        P("grp", "band", None, None),
        P("grp", "band"),
        P("sect", None),
        P(None, None, None, "sect", None),
        P(),
        P("sect", None),
        P(),
        P(),
        P(),
        P(),
        P(),
        P(),
        P(),
    )
    out_specs = P("grp", "band", None, None)
    return jax.shard_map(shards, mesh=mesh, in_specs=in_specs, out_specs=out_specs, check_vma=False)
```

```python
import functools

import jax
import jax.numpy as jnp
from jax import lax
from jax.experimental import pallas as pl
from jax.experimental.pallas import tpu as pltpu
from jax.sharding import PartitionSpec as P

DILATIONS = (12, 24, 36)
LAND_BLOCK = 6
LAND_MOST = 4
PRECISE = lax.Precision.HIGHEST
MESH = pl.DeviceIdType.MESH
F32 = jnp.float32
BF16 = jnp.bfloat16


def plan(rows, bands):
    off = []
    for k in (1, 2, 3):
        d = DILATIONS[k - 1]
        assert d % rows == 0
        hop = d // rows
        if hop < bands:
            off.append((k, 0, hop))
            off.append((k, 2, hop))
    order = [3, 2, 0, 1]
    return off, order


def kernel(
    dims, mask, feat_h, low_h, w1_h, wd_h, bbr, wpool_h, bpool, wproj_h, bproj, wr, br, wm_h, bm,
    out,
    feat, low, low_halo, w1, wd, wpool, wproj, wmp, wml, comp, m_l, m_r,
    part_off, crecv_off, xsend_off, xrecv_off, zsend, zrecv,
    part_own, crecv_own, xsend_own, xrecv_own, keep_off, keep_own,
    sums, pool_s, pool_b, gath, gath_b, halo, joined, lowred, lowacc, outc,
    loc_sem, lo_s, lo_r, c_s, c_r, x_s, x_r, z_s, z_r, ps_s, ps_r, pb_s, pb_r,
    gx_s, gx_r, gc_s, gc_r, hx_s, hx_r, hc_s, hc_r,
):
    mb, rows, cols, ch, br_w, live, nb, ns, low_w, lowp = dims
    nx = ns // 2
    cs = cols // nx
    off, order = plan(rows, nb)
    n_off = len(off)
    need = [(k, 1) for k in order if k] + [(k, i) for k, i, _ in off]
    pad = (m_l.shape[1] - cols) // 2

    band = lax.axis_index("band")
    sect = lax.axis_index("sect")
    core = lax.rem(sect, 2)
    xi = lax.div(sect, 2)

    locals_ = {}

    def fetch(name, src, dst):
        c = pltpu.make_async_copy(src, dst, loc_sem.at[len(locals_)])
        locals_[name] = c
        c.start()

    fetch("feat", feat_h, feat)
    for k, i, _ in off:
        fetch((k, i), wd_h.at[k - 1, i], wd.at[need.index((k, i))])
    fetch("wpool", wpool_h, wpool)
    for k in order:
        if k:
            fetch((k, 1), wd_h.at[k - 1, 1], wd.at[need.index((k, 1))])
        else:
            fetch("w1", w1_h, w1)
    fetch("low", low_h, low)
    fetch("wproj", wproj_h, wproj)
    fetch("wml", wm_h.at[:, :, pl.ds(br_w, lowp)], wml)
    for i in range(3):
        for j in range(3):
            fetch(("wmp", i, j), wm_h.at[i, j, pl.ds(0, br_w)], wmp.at[j, pl.ds(i * br_w, br_w)])

    bar = pltpu.get_barrier_semaphore()
    up_ok = band >= 1
    dn_ok = band + 1 < nb

    def hello(b, s):
        pl.semaphore_signal(bar, inc=1, device_id={"band": b, "sect": s}, device_id_type=MESH)

    for e in range(1, ns):
        hello(band, lax.rem(sect + e, ns))
    for e in range(1, nb):
        hello(lax.rem(band + e, nb), sect)
    for ok, step in ((up_ok, -1), (dn_ok, 1)):
        @pl.when(ok)
        def _(step=step):
            for e in range(1, nx):
                hello(band + step, lax.rem(sect + 2 * e, ns))
    def rcopy(src, dst, s, r, **where):
        return pltpu.make_async_remote_copy(
            src_ref=src, dst_ref=dst, send_sem=s, recv_sem=r, device_id=where, device_id_type=MESH
        )

    low_up = rcopy(low_h.at[:, 0], low_halo.at[1], lo_s.at[0], lo_r.at[1], band=band - 1, sect=sect)
    low_dn = rcopy(
        low_h.at[:, rows - 1], low_halo.at[0], lo_s.at[1], lo_r.at[0], band=band + 1, sect=sect
    )

    def slots(m):
        on = [mask[m, y] for y in range(rows)]
        slot_of = [jnp.int32(0)] + [None] * (rows - 2) + [jnp.int32(live - 1)]
        row_of = [jnp.int32(0)] * live
        row_of[live - 1] = jnp.int32(rows - 1)
        held = [jnp.int32(0)] * live
        held[0] = on[0]
        held[live - 1] = on[rows - 1]
        count = jnp.int32(0)
        for y in range(1, rows - 1):
            slot_of[y] = jnp.where(on[y] > 0, jnp.minimum(count + 1, live - 1), 0)
            for r in range(1, live - 1):
                hit = jnp.logical_and(on[y] > 0, count == r - 1)
                row_of[r] = jnp.where(hit, y, row_of[r])
                held[r] = jnp.where(hit, 1, held[r])
            count = count + on[y]
        return on, slot_of, row_of, held

    for ref in (m_l, m_r):
        zero = jnp.zeros((ref.shape[0], pad, br_w), F32)
        ref[:, :pad] = zero
        ref[:, pad + cols :] = zero
    for at in (0, rows + 1):
        joined[:, at] = jnp.zeros((mb, cols, br_w), BF16)

    locals_["feat"].wait()

    def taps(lhs, n, wref, d):
        mid = jnp.dot(lhs, wref[1], preferred_element_type=F32).reshape(n, cols, br_w)
        m_l[:n, pl.ds(pad, cols)] = jnp.dot(
            lhs, wref[0], preferred_element_type=F32
        ).reshape(n, cols, br_w)
        m_r[:n, pl.ds(pad, cols)] = jnp.dot(
            lhs, wref[2], preferred_element_type=F32
        ).reshape(n, cols, br_w)
        return mid + m_l[:n, pl.ds(pad - d, cols)] + m_r[:n, pl.ds(pad + d, cols)]

    def core_copy(t):
        if t < n_off:
            src, dst = part_off.at[t, 0], crecv_off.at[t]
        else:
            src, dst = part_own.at[t - n_off, 0], crecv_own.at[t - n_off]
        return rcopy(src, dst, c_s.at[t], c_r.at[t], sect=xi * 2 + 1 - core)

    def x_copy(t, e, incoming=False):
        send, recv, u = (
            (xsend_off, xrecv_off, t) if t < n_off else (xsend_own, xrecv_own, t - n_off)
        )
        other = lax.rem(xi + e, nx)
        slot = other if incoming else xi
        return rcopy(
            send.at[u, other], recv.at[u, slot], x_s.at[t, other], x_r.at[t, slot],
            sect=other * 2 + core,
        )

    def first(t):
        def body(step, carry):
            image = jnp.where(step == 0, 1 - core, core)
            if t < n_off:
                k, i, _ = off[t]
                lhs = feat[image].reshape(rows * cols, ch)
                val = taps(lhs, rows, wd.at[need.index((k, i))], DILATIONS[k - 1])
                part_off[t, step] = val.astype(BF16)
            else:
                k = order[t - n_off]
                lhs = comp[image].reshape(live * cols, ch)
                if k:
                    val = taps(lhs, live, wd.at[need.index((k, 1))], DILATIONS[k - 1])
                else:
                    val = jnp.dot(lhs, w1[...], preferred_element_type=F32).reshape(
                        live, cols, br_w
                    )
                part_own[t - n_off, step] = val.astype(BF16)

            if t >= n_off:
                @pl.when(step == 0)
                def _():
                    core_copy(t).start()
            return carry

        lax.fori_loop(0, 2, body, 0)

    def second(t):
        core_copy(t).wait_recv()
        part, got, send, keep, u = (
            (part_off, crecv_off, xsend_off, keep_off, t)
            if t < n_off
            else (part_own, crecv_own, xsend_own, keep_own, t - n_off)
        )
        for c in range(nx):
            cell = pl.ds(c * cs, cs)
            total = part[u, 1, :, cell].astype(F32) + got[u, :, cell].astype(F32)
            send[u, c] = total.astype(BF16)

            @pl.when(xi == c)
            def _():
                keep[u] = total
        for e in range(1, nx):
            x_copy(t, e).start()

    def shared(t):
        recv, keep, u = (
            (xrecv_off, keep_off, t) if t < n_off else (xrecv_own, keep_own, t - n_off)
        )
        total = keep[u]
        for e in range(1, nx):
            x_copy(t, e, True).wait_recv()
            total = total + recv[u, lax.rem(xi + e, nx)].astype(F32)
        return total

    def sends_to(t):
        k, i, hop = off[t]
        return band + hop < nb if i == 0 else band - hop >= 0

    def gets_from(t):
        k, i, hop = off[t]
        return band - hop >= 0 if i == 0 else band + hop < nb

    def z_copy(t):
        k, i, hop = off[t]
        return rcopy(
            zsend.at[t], zrecv.at[t], z_s.at[t], z_r.at[t],
            band=band + hop if i == 0 else band - hop, sect=sect,
        )

    def third_off(t):
        zsend[t] = shared(t).astype(BF16)
        z_copy(t).start()

    def guarded(fn, t):
        @pl.when(sends_to(t))
        def _():
            fn(t)

    for t in range(n_off):
        locals_[off[t][:2]].wait()
        guarded(first, t)

    sides_held = jnp.minimum(band, 1) + jnp.minimum(nb - 1 - band, 1)
    pl.semaphore_wait(bar, (ns - 1) + (nb - 1) + (nx - 1) * sides_held)

    for t in range(n_off):
        guarded(lambda t: core_copy(t).start(), t)
    @pl.when(up_ok)
    def _():
        low_up.start()

    @pl.when(dn_ok)
    def _():
        low_dn.start()

    sums[...] = jnp.zeros_like(sums)
    locals_["wpool"].wait()
    for m in range(mb):
        acc = jnp.zeros((cols, ch), F32)
        for y in range(rows):
            acc = acc + feat[m, y].astype(F32)
        sums[m : m + 1, :] = jnp.sum(acc, axis=0, keepdims=True)
    pool_s[sect] = jnp.dot(
        sums[...], wpool[...].astype(F32), precision=PRECISE, preferred_element_type=F32
    )

    def pool_sect(e, incoming=False):
        other = lax.rem(sect + e, ns)
        slot = other if incoming else sect
        return rcopy(
            pool_s.at[sect], pool_s.at[slot], ps_s.at[other], ps_r.at[slot], sect=other
        )

    def pool_band(e, incoming=False):
        other = lax.rem(band + e, nb)
        slot = other if incoming else band
        return rcopy(
            pool_b.at[band], pool_b.at[slot], pb_s.at[other], pb_r.at[slot], band=other
        )

    for e in range(1, ns):
        pool_sect(e).start()

    facts = [slots(m) for m in range(mb)]
    for m in range(mb):
        for r in range(live):
            comp[m, r] = feat[m, facts[m][2][r]]

    for t in range(n_off):
        guarded(second, t)

    t0 = n_off

    def own(u):
        locals_[(order[u], 1) if order[u] else "w1"].wait()
        first(t0 + u)

    own(0)
    own(1)
    second(t0)
    for e in range(1, ns):
        pool_sect(e, True).wait_recv()
    total = pool_s[0]
    for s in range(1, ns):
        total = total + pool_s[s]
    pool_b[band] = total
    for e in range(1, nb):
        pool_band(e).start()

    own(2)
    second(t0 + 1)
    own(3)
    second(t0 + 2)
    for t in range(n_off):
        guarded(third_off, t)
    second(t0 + 3)

    locals_["low"].wait()
    locals_["wml"].wait()

    def reduced(v):
        return jax.nn.relu(
            lax.dot_general(
                v, wr[...], (((1,), (1,)), ((), ())), preferred_element_type=F32
            )
            + br[...]
        ).astype(BF16)

    for m in range(mb):
        lowred[m, 1 : rows + 1] = reduced(low[m].reshape(rows * cols, low_w)).reshape(
            rows, cols, lowp
        )
    for side, at, ok, copy in ((0, 0, up_ok, low_dn), (1, rows + 1, dn_ok, low_up)):
        @pl.when(ok)
        def _(side=side, at=at, copy=copy):
            copy.wait_recv()
            for m in range(mb):
                lowred[m, at] = reduced(low_halo[side, m])

        @pl.when(jnp.logical_not(ok))
        def _(at=at):
            for m in range(mb):
                lowred[m, at] = jnp.zeros((cols, lowp), BF16)

    def stash(terms):
        for ref, term in zip((m_l, m_r), (terms[0], terms[2])):
            ref[:live, pl.ds(pad, cols)] = term.reshape(live, cols, br_w)
        outc[...] = terms[1].reshape(live, cols, br_w)

    def combined():
        return outc[...] + m_l[:live, pl.ds(pad - 1, cols)] + m_r[:live, pl.ds(pad + 1, cols)]

    for m in range(mb):
        row_of = facts[m][2]
        terms = [None] * 3
        for i in range(3):
            lhs = jnp.concatenate([lowred[m, row_of[r] + i] for r in range(live)], axis=0)
            for j in range(3):
                term = jnp.dot(lhs, wml[i, j], preferred_element_type=F32)
                terms[j] = term if i == 0 else terms[j] + term
        stash(terms)
        lowacc[m] = combined() + bm[...].reshape(1, 1, br_w)

    locals_["wproj"].wait()
    for e in range(1, nb):
        pool_band(e, True).wait_recv()
    total = pool_b[0]
    for b in range(1, nb):
        total = total + pool_b[b]
    pooled = jax.nn.relu(total / (nb * rows * cols) + bpool[...])
    context = jnp.dot(
        pooled, wproj[4 * br_w :].astype(F32), precision=PRECISE, preferred_element_type=F32
    )
    mine = context[0:1]
    for m in range(1, mb):
        mine = jnp.where(core == m, context[m : m + 1], mine)
    base = mine + bproj[...]

    _, _, own_row, own_held = slots(core)
    acc = jnp.zeros((live * cs, br_w), F32)
    for u, k in enumerate(order):
        keep_own[u] = shared(t0 + u)
        for t in range(n_off):
            if off[t][0] == k:
                @pl.when(gets_from(t))
                def _(t=t, u=u):
                    z_copy(t).wait_recv()
                    for r in range(live):
                        keep_own[u, r] = keep_own[u, r] + zrecv[t, own_row[r]].astype(F32)
        branch = jax.nn.relu(keep_own[u] + bbr[k : k + 1].reshape(1, 1, br_w)).astype(BF16)
        acc = acc + jnp.dot(
            branch.reshape(live * cs, br_w), wproj[k * br_w : (k + 1) * br_w],
            preferred_element_type=F32,
        )
    done = jax.nn.relu(acc + base).reshape(live, cs, br_w)
    for r in range(live):
        gath[xi, r] = (done[r] * own_held[r].astype(F32)).astype(BF16)

    peer = xi * 2 + 1 - core

    def gather_x(e, incoming=False):
        other = lax.rem(xi + e, nx)
        slot = other if incoming else xi
        return rcopy(
            gath.at[xi], gath.at[slot], gx_s.at[other], gx_r.at[slot], sect=other * 2 + core
        )

    def gather_core(c):
        return rcopy(gath.at[c], gath_b.at[c], gc_s.at[c], gc_r.at[c], sect=peer)

    def halo_x(side, e, incoming=False):
        other = lax.rem(xi + e, nx)
        slot = other if incoming else xi
        src = gath.at[xi, live - 1 if side == 0 else 0]
        return rcopy(
            src, halo.at[side, slot * 2 + core], hx_s.at[side, other], hx_r.at[side, slot],
            band=band + 1 if side == 0 else band - 1, sect=other * 2 + core,
        )

    def halo_core(side, c, incoming=False):
        cell = c * 2 + (1 - core if incoming else core)
        return rcopy(
            halo.at[side, cell], halo.at[side, cell], hc_s.at[side, c], hc_r.at[side, c], sect=peer
        )

    for e in range(1, nx):
        gather_x(e).start()
    for side, ok in ((0, dn_ok), (1, up_ok)):
        @pl.when(ok)
        def _(side=side):
            for e in range(nx):
                halo_x(side, e).start()
    gather_core(xi).start()
    for i in range(3):
        for j in range(3):
            locals_[("wmp", i, j)].wait()
    for e in range(1, nx):
        gather_x(e, True).wait_recv()
        gather_core(lax.rem(xi + e, nx)).start()

    for step in range(2):
        image = core if step == 0 else 1 - core
        on, slot_of, row_of, _ = slots(image)
        cells = gath if step == 0 else gath_b
        if step == 1:
            for c in range(nx):
                gather_core(c).wait_recv()
        for y in range(rows):
            for c in range(nx):
                joined[image, y + 1, pl.ds(c * cs, cs)] = (
                    cells[c, slot_of[y]].astype(F32) * on[y].astype(F32)
                ).astype(BF16)
        lhs = jnp.concatenate(
            [
                jnp.concatenate([joined[image, row_of[r] + i] for r in range(live)], axis=0)
                for i in range(3)
            ],
            axis=1,
        )
        stash([jnp.dot(lhs, wmp[j], preferred_element_type=F32) for j in range(3)])
        for side, ok in ((0, up_ok), (1, dn_ok)):
            @pl.when(ok)
            def _(side=side, step=step, image=image):
                for e in range(nx):
                    if step == 0:
                        halo_x(side, e, True).wait_recv()
                        halo_core(side, lax.rem(xi + e, nx)).start()
                    else:
                        halo_core(side, e, True).wait_recv()
                edge = jnp.concatenate([halo[side, c * 2 + image] for c in range(nx)], axis=0)
                at = 0 if side == 0 else live - 1
                tap = pl.ds(2 * br_w * side, br_w)
                add = [
                    jnp.dot(edge, wmp[j, tap], preferred_element_type=F32) for j in range(3)
                ]
                m_l[at, pl.ds(pad, cols)] = m_l[at, pl.ds(pad, cols)] + add[0]
                outc[at] = outc[at] + add[1]
                m_r[at, pl.ds(pad, cols)] = m_r[at, pl.ds(pad, cols)] + add[2]
        outc[...] = jax.nn.relu(combined() + lowacc[image])
        for y in range(rows):
            out[image, y] = outc[slot_of[y]].astype(BF16)

    @pl.when(up_ok)
    def _():
        low_up.wait_send()

    @pl.when(dn_ok)
    def _():
        low_dn.wait_send()

    def left(t):
        core_copy(t).wait_send()
        for e in range(1, nx):
            x_copy(t, e).wait_send()

    for t in range(n_off):
        guarded(left, t)
        guarded(lambda t: z_copy(t).wait_send(), t)
    for u in range(4):
        left(t0 + u)
    for e in range(1, ns):
        pool_sect(e).wait_send()
    for e in range(1, nb):
        pool_band(e).wait_send()
    for e in range(1, nx):
        gather_x(e).wait_send()
    for c in range(nx):
        gather_core(c).wait_send()
    for side, ok in ((0, dn_ok), (1, up_ok)):
        @pl.when(ok)
        def _(side=side):
            for e in range(nx):
                halo_x(side, e).wait_send()
    for side, ok in ((0, up_ok), (1, dn_ok)):
        @pl.when(ok)
        def _(side=side):
            for c in range(nx):
                halo_core(side, c).wait_send()


def shards(
    features, low_level, land_mask, weight_one, weight_dilated, bias_branch, weight_pool,
    bias_pool, weight_project, bias_project, weight_reduce, bias_reduce, weight_merging,
    bias_merging,
):
    mb, rows, cols, ch = features.shape
    br_w = weight_project.shape[1]
    low_w, lowp = weight_reduce.shape
    nb, ns = lax.axis_size("band"), lax.axis_size("sect")
    nx = ns // 2
    cs = cols // nx
    assert mb == 2 and ns % 2 == 0
    live = rows // LAND_BLOCK * LAND_MOST if rows % LAND_BLOCK == 0 else rows
    off, order = plan(rows, nb)
    n_off = max(len(off), 1)
    n_all = len(off) + 4
    pad = -(-max(DILATIONS) // 8) * 8
    vm, dma = pltpu.VMEM, pltpu.SemaphoreType.DMA
    dims = (mb, rows, cols, ch, br_w, live, nb, ns, low_w, lowp)
    scratch = [
        vm(features.shape, BF16),
        vm(low_level.shape, BF16),
        vm((2, mb, cols, low_w), BF16),
        vm(weight_one.shape, BF16),
        vm((3 + len(off), 3, ch, br_w), BF16),
        vm(weight_pool.shape, BF16),
        vm(weight_project.shape, BF16),
        vm((3, 3 * br_w, weight_merging.shape[3]), BF16),
        vm((3, 3, lowp, weight_merging.shape[3]), BF16),
        vm((mb, live, cols, ch), BF16),
        vm((rows, cols + 2 * pad, br_w), F32),
        vm((rows, cols + 2 * pad, br_w), F32),
        vm((n_off, 2, rows, cols, br_w), BF16),
        vm((n_off, rows, cols, br_w), BF16),
        vm((n_off, nx, rows, cs, br_w), BF16),
        vm((n_off, nx, rows, cs, br_w), BF16),
        vm((n_off, rows, cs, br_w), BF16),
        vm((n_off, rows, cs, br_w), BF16),
        vm((4, 2, live, cols, br_w), BF16),
        vm((4, live, cols, br_w), BF16),
        vm((4, nx, live, cs, br_w), BF16),
        vm((4, nx, live, cs, br_w), BF16),
        vm((n_off, rows, cs, br_w), F32),
        vm((4, live, cs, br_w), F32),
        vm((8, ch), F32),
        vm((ns, 8, br_w), F32),
        vm((nb, 8, br_w), F32),
        vm((nx, live, cs, br_w), BF16),
        vm((nx, live, cs, br_w), BF16),
        vm((2, ns, cs, br_w), BF16),
        vm((mb, rows + 2, cols, br_w), BF16),
        vm((mb, rows + 2, cols, lowp), BF16),
        vm((mb, live, cols, br_w), F32),
        vm((live, cols, br_w), F32),
        dma((19 + len(off),)),
        dma((2,)),
        dma((2,)),
        dma((n_all,)),
        dma((n_all,)),
        dma((n_all, nx)),
        dma((n_all, nx)),
        dma((n_off,)),
        dma((n_off,)),
        dma((ns,)),
        dma((ns,)),
        dma((nb,)),
        dma((nb,)),
        dma((nx,)),
        dma((nx,)),
        dma((nx,)),
        dma((nx,)),
        dma((2, nx)),
        dma((2, nx)),
        dma((2, nx)),
        dma((2, nx)),
    ]
    anym = pl.BlockSpec(memory_space=pl.ANY)
    vmem = pl.BlockSpec(memory_space=pltpu.VMEM)
    smem = pl.BlockSpec(memory_space=pltpu.SMEM)
    merged_map = pl.pallas_call(
        functools.partial(kernel, dims),
        out_shape=jax.ShapeDtypeStruct((mb, rows, cols, weight_merging.shape[3]), BF16),
        in_specs=[
            smem, anym, anym, anym, anym, vmem, anym, vmem, anym, vmem, vmem, vmem, anym, vmem,
        ],
        out_specs=vmem,
        scratch_shapes=scratch,
        compiler_params=pltpu.CompilerParams(
            collective_id=0, has_side_effects=True, vmem_limit_bytes=60 * 1024 * 1024
        ),
    )(
        land_mask, features, low_level, weight_one, weight_dilated, bias_branch, weight_pool,
        bias_pool.reshape(1, -1), weight_project, bias_project.reshape(1, -1), weight_reduce.T,
        bias_reduce.reshape(1, -1), weight_merging, bias_merging.reshape(1, -1),
    )
    return jnp.where(land_mask[:, :, None, None] != 0, merged_map, jnp.zeros_like(merged_map))


def solution(mesh):
    in_specs = (
        P("grp", "band", None, "sect"),
        P("grp", "band", None, None),
        P("grp", "band"),
        P("sect", None),
        P(None, None, None, "sect", None),
        P(),
        P("sect", None),
        P(),
        P(),
        P(),
        P(),
        P(),
        P(),
        P(),
    )
    out_specs = P("grp", "band", None, None)
    return jax.shard_map(shards, mesh=mesh, in_specs=in_specs, out_specs=out_specs, check_vma=False)
```

```python
import functools

import jax
import jax.numpy as jnp
from jax import lax
from jax.experimental import pallas as pl
from jax.experimental.pallas import tpu as pltpu
from jax.sharding import PartitionSpec as P

DILATIONS = (12, 24, 36)
LAND_BLOCK = 6
LAND_MOST = 4
PRECISE = lax.Precision.HIGHEST
MESH = pl.DeviceIdType.MESH
F32 = jnp.float32
BF16 = jnp.bfloat16


def plan(rows, bands):
    off = []
    for k in (1, 2, 3):
        d = DILATIONS[k - 1]
        assert d % rows == 0
        hop = d // rows
        if hop < bands:
            off.append((k, 0, hop))
            off.append((k, 2, hop))
    order = [3, 2, 0, 1]
    return off, order


def kernel(
    dims, mask, feat_h, low_h, w1_h, wd_h, bbr, wpool_h, bpool, wproj_h, bproj, wr, br, wm_h, bm,
    out,
    feat, low, low_halo, w1, wd, wpool, wproj, wmp, wml, comp, m_l, m_r,
    part_off, crecv_off, xsend_off, xrecv_off, zsend, zrecv,
    part_own, crecv_own, xsend_own, xrecv_own, keep_off, keep_own,
    sel, sel_got, sums, pool_s, pool_b, gath, gath_b, halo, joined, lowred, lowacc, outc,
    loc_sem, se_s, se_r, lo_s, lo_r, c_s, c_r, x_s, x_r, z_s, z_r, ps_s, ps_r, pb_s, pb_r,
    gx_s, gx_r, gc_s, gc_r, hx_s, hx_r, hc_s, hc_r,
):
    mb, rows, cols, ch, br_w, live, nb, ns, low_w, lowp = dims
    nx = ns // 2
    cs = cols // nx
    off, order = plan(rows, nb)
    n_off = len(off)
    need = [(k, 1) for k in order if k] + [(k, i) for k, i, _ in off]
    pad = (m_l.shape[1] - cols) // 2

    band = lax.axis_index("band")
    sect = lax.axis_index("sect")
    core = lax.rem(sect, 2)
    xi = lax.div(sect, 2)

    locals_ = {}

    def fetch(name, src, dst):
        c = pltpu.make_async_copy(src, dst, loc_sem.at[len(locals_)])
        locals_[name] = c
        c.start()

    fetch("feat", feat_h, feat)
    for k, i, _ in off:
        fetch((k, i), wd_h.at[k - 1, i], wd.at[need.index((k, i))])
    fetch("wpool", wpool_h, wpool)
    for k in order:
        if k:
            fetch((k, 1), wd_h.at[k - 1, 1], wd.at[need.index((k, 1))])
        else:
            fetch("w1", w1_h, w1)
    fetch("low", low_h, low)
    fetch("wproj", wproj_h, wproj)
    fetch("wml", wm_h.at[:, :, pl.ds(br_w, lowp)], wml)
    for i in range(3):
        for j in range(3):
            fetch(("wmp", i, j), wm_h.at[i, j, pl.ds(0, br_w)], wmp.at[j, pl.ds(i * br_w, br_w)])

    bar = pltpu.get_barrier_semaphore()
    up_ok = band >= 1
    dn_ok = band + 1 < nb

    def hello(b, s):
        pl.semaphore_signal(bar, inc=1, device_id={"band": b, "sect": s}, device_id_type=MESH)

    for e in range(1, ns):
        hello(band, lax.rem(sect + e, ns))
    for e in range(1, nb):
        hello(lax.rem(band + e, nb), sect)
    for ok, step in ((up_ok, -1), (dn_ok, 1)):
        @pl.when(ok)
        def _(step=step):
            for e in range(1, nx):
                hello(band + step, lax.rem(sect + 2 * e, ns))
    def rcopy(src, dst, s, r, **where):
        return pltpu.make_async_remote_copy(
            src_ref=src, dst_ref=dst, send_sem=s, recv_sem=r, device_id=where, device_id_type=MESH
        )

    low_up = rcopy(low_h.at[:, 0], low_halo.at[1], lo_s.at[0], lo_r.at[1], band=band - 1, sect=sect)
    low_dn = rcopy(
        low_h.at[:, rows - 1], low_halo.at[0], lo_s.at[1], lo_r.at[0], band=band + 1, sect=sect
    )

    def slots(m):
        on = [mask[m, y] for y in range(rows)]
        slot_of = [jnp.int32(0)] + [None] * (rows - 2) + [jnp.int32(live - 1)]
        row_of = [jnp.int32(0)] * live
        row_of[live - 1] = jnp.int32(rows - 1)
        held = [jnp.int32(0)] * live
        held[0] = on[0]
        held[live - 1] = on[rows - 1]
        count = jnp.int32(0)
        for y in range(1, rows - 1):
            slot_of[y] = jnp.where(on[y] > 0, jnp.minimum(count + 1, live - 1), 0)
            for r in range(1, live - 1):
                hit = jnp.logical_and(on[y] > 0, count == r - 1)
                row_of[r] = jnp.where(hit, y, row_of[r])
                held[r] = jnp.where(hit, 1, held[r])
            count = count + on[y]
        return on, slot_of, row_of, held

    for ref in (m_l, m_r):
        zero = jnp.zeros((ref.shape[0], pad, br_w), F32)
        ref[:, :pad] = zero
        ref[:, pad + cols :] = zero
    for at in (0, rows + 1):
        joined[:, at] = jnp.zeros((mb, cols, br_w), BF16)

    _, _, own_row, own_held = slots(core)
    sel[...] = jnp.zeros_like(sel)
    for r in range(1, live - 1):
        for y in range(1, rows - 1):
            sel[r, pl.ds(y, 1)] = jnp.where(
                own_row[r] == y, jnp.ones((1, br_w), F32), jnp.zeros((1, br_w), F32)
            )

    locals_["feat"].wait()

    def taps(lhs, n, wref, d):
        mid = jnp.dot(lhs, wref[1], preferred_element_type=F32).reshape(n, cols, br_w)
        m_l[:n, pl.ds(pad, cols)] = jnp.dot(
            lhs, wref[0], preferred_element_type=F32
        ).reshape(n, cols, br_w)
        m_r[:n, pl.ds(pad, cols)] = jnp.dot(
            lhs, wref[2], preferred_element_type=F32
        ).reshape(n, cols, br_w)
        return mid + m_l[:n, pl.ds(pad - d, cols)] + m_r[:n, pl.ds(pad + d, cols)]

    def core_copy(t):
        if t < n_off:
            src, dst = part_off.at[t, 0], crecv_off.at[t]
        else:
            src, dst = part_own.at[t - n_off, 0], crecv_own.at[t - n_off]
        return rcopy(src, dst, c_s.at[t], c_r.at[t], sect=xi * 2 + 1 - core)

    def x_copy(t, e, incoming=False):
        send, recv, u = (
            (xsend_off, xrecv_off, t) if t < n_off else (xsend_own, xrecv_own, t - n_off)
        )
        other = lax.rem(xi + e, nx)
        slot = other if incoming else xi
        return rcopy(
            send.at[u, other], recv.at[u, slot], x_s.at[t, other], x_r.at[t, slot],
            sect=other * 2 + core,
        )

    def first(t):
        def body(step, carry):
            image = jnp.where(step == 0, 1 - core, core)
            if t < n_off:
                k, i, _ = off[t]
                lhs = feat[image].reshape(rows * cols, ch)
                val = taps(lhs, rows, wd.at[need.index((k, i))], DILATIONS[k - 1])
                part_off[t, step] = val.astype(BF16)
            else:
                k = order[t - n_off]
                lhs = comp[image].reshape(live * cols, ch)
                if k:
                    val = taps(lhs, live, wd.at[need.index((k, 1))], DILATIONS[k - 1])
                else:
                    val = jnp.dot(lhs, w1[...], preferred_element_type=F32).reshape(
                        live, cols, br_w
                    )
                part_own[t - n_off, step] = val.astype(BF16)

            if t >= n_off:
                @pl.when(step == 0)
                def _():
                    core_copy(t).start()
            return carry

        lax.fori_loop(0, 2, body, 0)

    def second(t):
        core_copy(t).wait_recv()
        if t < n_off:
            sel_copy(t).wait_recv()
        part, got, send, keep, u = (
            (part_off, crecv_off, xsend_off, keep_off, t)
            if t < n_off
            else (part_own, crecv_own, xsend_own, keep_own, t - n_off)
        )
        for c in range(nx):
            cell = pl.ds(c * cs, cs)
            total = part[u, 1, :, cell].astype(F32) + got[u, :, cell].astype(F32)
            if t < n_off:
                kept = [total[0]]
                for r in range(1, live - 1):
                    row = jnp.zeros((cs, br_w), F32)
                    for y in range(1, rows - 1):
                        row = row + sel_got[u, r, pl.ds(y, 1)] * total[y]
                    kept.append(row)
                total = jnp.stack(kept + [total[rows - 1]], axis=0)
            send[u, c] = total.astype(BF16)

            @pl.when(xi == c)
            def _():
                keep[u] = total
        for e in range(1, nx):
            x_copy(t, e).start()

    def shared(t):
        recv, keep, u = (
            (xrecv_off, keep_off, t) if t < n_off else (xrecv_own, keep_own, t - n_off)
        )
        total = keep[u]
        for e in range(1, nx):
            x_copy(t, e, True).wait_recv()
            total = total + recv[u, lax.rem(xi + e, nx)].astype(F32)
        return total

    def sends_to(t):
        k, i, hop = off[t]
        return band + hop < nb if i == 0 else band - hop >= 0

    def gets_from(t):
        k, i, hop = off[t]
        return band - hop >= 0 if i == 0 else band + hop < nb

    def z_copy(t):
        k, i, hop = off[t]
        return rcopy(
            zsend.at[t], zrecv.at[t], z_s.at[t], z_r.at[t],
            band=band + hop if i == 0 else band - hop, sect=sect,
        )

    def sel_copy(t):
        k, i, hop = off[t]
        return rcopy(
            sel, sel_got.at[t], se_s.at[t], se_r.at[t],
            band=band - hop if i == 0 else band + hop, sect=sect,
        )

    def third_off(t):
        zsend[t] = shared(t).astype(BF16)
        z_copy(t).start()

    def guarded(fn, t):
        @pl.when(sends_to(t))
        def _():
            fn(t)

    for t in range(n_off):
        locals_[off[t][:2]].wait()
        guarded(first, t)

    sides_held = jnp.minimum(band, 1) + jnp.minimum(nb - 1 - band, 1)
    pl.semaphore_wait(bar, (ns - 1) + (nb - 1) + (nx - 1) * sides_held)

    for t in range(n_off):
        guarded(lambda t: core_copy(t).start(), t)
    for t in range(n_off):
        @pl.when(gets_from(t))
        def _(t=t):
            sel_copy(t).start()
    @pl.when(up_ok)
    def _():
        low_up.start()

    @pl.when(dn_ok)
    def _():
        low_dn.start()

    sums[...] = jnp.zeros_like(sums)
    locals_["wpool"].wait()
    for m in range(mb):
        acc = jnp.zeros((cols, ch), F32)
        for y in range(rows):
            acc = acc + feat[m, y].astype(F32)
        sums[m : m + 1, :] = jnp.sum(acc, axis=0, keepdims=True)
    pool_s[sect] = jnp.dot(
        sums[...], wpool[...].astype(F32), precision=PRECISE, preferred_element_type=F32
    )

    def pool_sect(e, incoming=False):
        other = lax.rem(sect + e, ns)
        slot = other if incoming else sect
        return rcopy(
            pool_s.at[sect], pool_s.at[slot], ps_s.at[other], ps_r.at[slot], sect=other
        )

    def pool_band(e, incoming=False):
        other = lax.rem(band + e, nb)
        slot = other if incoming else band
        return rcopy(
            pool_b.at[band], pool_b.at[slot], pb_s.at[other], pb_r.at[slot], band=other
        )

    for e in range(1, ns):
        pool_sect(e).start()

    facts = [slots(m) for m in range(mb)]
    for m in range(mb):
        for r in range(live):
            comp[m, r] = feat[m, facts[m][2][r]]

    for t in range(n_off):
        guarded(second, t)

    t0 = n_off

    def own(u):
        locals_[(order[u], 1) if order[u] else "w1"].wait()
        first(t0 + u)

    own(0)
    own(1)
    second(t0)
    for e in range(1, ns):
        pool_sect(e, True).wait_recv()
    total = pool_s[0]
    for s in range(1, ns):
        total = total + pool_s[s]
    pool_b[band] = total
    for e in range(1, nb):
        pool_band(e).start()

    own(2)
    second(t0 + 1)
    own(3)
    second(t0 + 2)
    for t in range(n_off):
        guarded(third_off, t)
    second(t0 + 3)

    locals_["low"].wait()
    locals_["wml"].wait()

    def reduced(v):
        return jax.nn.relu(
            lax.dot_general(
                v, wr[...], (((1,), (1,)), ((), ())), preferred_element_type=F32
            )
            + br[...]
        ).astype(BF16)

    for m in range(mb):
        lowred[m, 1 : rows + 1] = reduced(low[m].reshape(rows * cols, low_w)).reshape(
            rows, cols, lowp
        )
    for side, at, ok, copy in ((0, 0, up_ok, low_dn), (1, rows + 1, dn_ok, low_up)):
        @pl.when(ok)
        def _(side=side, at=at, copy=copy):
            copy.wait_recv()
            for m in range(mb):
                lowred[m, at] = reduced(low_halo[side, m])

        @pl.when(jnp.logical_not(ok))
        def _(at=at):
            for m in range(mb):
                lowred[m, at] = jnp.zeros((cols, lowp), BF16)

    def stash(terms):
        for ref, term in zip((m_l, m_r), (terms[0], terms[2])):
            ref[:live, pl.ds(pad, cols)] = term.reshape(live, cols, br_w)
        outc[...] = terms[1].reshape(live, cols, br_w)

    def combined():
        return outc[...] + m_l[:live, pl.ds(pad - 1, cols)] + m_r[:live, pl.ds(pad + 1, cols)]

    for m in range(mb):
        row_of = facts[m][2]
        terms = [None] * 3
        for i in range(3):
            lhs = jnp.concatenate([lowred[m, row_of[r] + i] for r in range(live)], axis=0)
            for j in range(3):
                term = jnp.dot(lhs, wml[i, j], preferred_element_type=F32)
                terms[j] = term if i == 0 else terms[j] + term
        stash(terms)
        lowacc[m] = combined() + bm[...].reshape(1, 1, br_w)

    locals_["wproj"].wait()
    for e in range(1, nb):
        pool_band(e, True).wait_recv()
    total = pool_b[0]
    for b in range(1, nb):
        total = total + pool_b[b]
    pooled = jax.nn.relu(total / (nb * rows * cols) + bpool[...])
    context = jnp.dot(
        pooled, wproj[4 * br_w :].astype(F32), precision=PRECISE, preferred_element_type=F32
    )
    mine = context[0:1]
    for m in range(1, mb):
        mine = jnp.where(core == m, context[m : m + 1], mine)
    base = mine + bproj[...]

    acc = jnp.zeros((live * cs, br_w), F32)
    for u, k in enumerate(order):
        keep_own[u] = shared(t0 + u)
        for t in range(n_off):
            if off[t][0] == k:
                @pl.when(gets_from(t))
                def _(t=t, u=u):
                    z_copy(t).wait_recv()
                    keep_own[u] = keep_own[u] + zrecv[t].astype(F32)
        branch = jax.nn.relu(keep_own[u] + bbr[k : k + 1].reshape(1, 1, br_w)).astype(BF16)
        acc = acc + jnp.dot(
            branch.reshape(live * cs, br_w), wproj[k * br_w : (k + 1) * br_w],
            preferred_element_type=F32,
        )
    done = jax.nn.relu(acc + base).reshape(live, cs, br_w)
    for r in range(live):
        gath[xi, r] = (done[r] * own_held[r].astype(F32)).astype(BF16)

    peer = xi * 2 + 1 - core

    def gather_x(e, incoming=False):
        other = lax.rem(xi + e, nx)
        slot = other if incoming else xi
        return rcopy(
            gath.at[xi], gath.at[slot], gx_s.at[other], gx_r.at[slot], sect=other * 2 + core
        )

    def gather_core(c):
        return rcopy(gath.at[c], gath_b.at[c], gc_s.at[c], gc_r.at[c], sect=peer)

    def halo_x(side, e, incoming=False):
        other = lax.rem(xi + e, nx)
        slot = other if incoming else xi
        src = gath.at[xi, live - 1 if side == 0 else 0]
        return rcopy(
            src, halo.at[side, slot * 2 + core], hx_s.at[side, other], hx_r.at[side, slot],
            band=band + 1 if side == 0 else band - 1, sect=other * 2 + core,
        )

    def halo_core(side, c, incoming=False):
        cell = c * 2 + (1 - core if incoming else core)
        return rcopy(
            halo.at[side, cell], halo.at[side, cell], hc_s.at[side, c], hc_r.at[side, c], sect=peer
        )

    for e in range(1, nx):
        gather_x(e).start()
    for side, ok in ((0, dn_ok), (1, up_ok)):
        @pl.when(ok)
        def _(side=side):
            for e in range(nx):
                halo_x(side, e).start()
    gather_core(xi).start()
    for i in range(3):
        for j in range(3):
            locals_[("wmp", i, j)].wait()
    for e in range(1, nx):
        gather_x(e, True).wait_recv()
        gather_core(lax.rem(xi + e, nx)).start()

    for step in range(2):
        image = core if step == 0 else 1 - core
        on, slot_of, row_of, _ = slots(image)
        cells = gath if step == 0 else gath_b
        if step == 1:
            for c in range(nx):
                gather_core(c).wait_recv()
        for y in range(rows):
            for c in range(nx):
                joined[image, y + 1, pl.ds(c * cs, cs)] = (
                    cells[c, slot_of[y]].astype(F32) * on[y].astype(F32)
                ).astype(BF16)
        lhs = jnp.concatenate(
            [
                jnp.concatenate([joined[image, row_of[r] + i] for r in range(live)], axis=0)
                for i in range(3)
            ],
            axis=1,
        )
        stash([jnp.dot(lhs, wmp[j], preferred_element_type=F32) for j in range(3)])
        for side, ok in ((0, up_ok), (1, dn_ok)):
            @pl.when(ok)
            def _(side=side, step=step, image=image):
                for e in range(nx):
                    if step == 0:
                        halo_x(side, e, True).wait_recv()
                        halo_core(side, lax.rem(xi + e, nx)).start()
                    else:
                        halo_core(side, e, True).wait_recv()
                edge = jnp.concatenate([halo[side, c * 2 + image] for c in range(nx)], axis=0)
                at = 0 if side == 0 else live - 1
                tap = pl.ds(2 * br_w * side, br_w)
                add = [
                    jnp.dot(edge, wmp[j, tap], preferred_element_type=F32) for j in range(3)
                ]
                m_l[at, pl.ds(pad, cols)] = m_l[at, pl.ds(pad, cols)] + add[0]
                outc[at] = outc[at] + add[1]
                m_r[at, pl.ds(pad, cols)] = m_r[at, pl.ds(pad, cols)] + add[2]
        outc[...] = jax.nn.relu(combined() + lowacc[image])
        for y in range(rows):
            out[image, y] = outc[slot_of[y]].astype(BF16)

    @pl.when(up_ok)
    def _():
        low_up.wait_send()

    @pl.when(dn_ok)
    def _():
        low_dn.wait_send()

    def left(t):
        core_copy(t).wait_send()
        for e in range(1, nx):
            x_copy(t, e).wait_send()

    for t in range(n_off):
        @pl.when(gets_from(t))
        def _(t=t):
            sel_copy(t).wait_send()

        guarded(left, t)
        guarded(lambda t: z_copy(t).wait_send(), t)
    for u in range(4):
        left(t0 + u)
    for e in range(1, ns):
        pool_sect(e).wait_send()
    for e in range(1, nb):
        pool_band(e).wait_send()
    for e in range(1, nx):
        gather_x(e).wait_send()
    for c in range(nx):
        gather_core(c).wait_send()
    for side, ok in ((0, dn_ok), (1, up_ok)):
        @pl.when(ok)
        def _(side=side):
            for e in range(nx):
                halo_x(side, e).wait_send()
    for side, ok in ((0, up_ok), (1, dn_ok)):
        @pl.when(ok)
        def _(side=side):
            for c in range(nx):
                halo_core(side, c).wait_send()


def shards(
    features, low_level, land_mask, weight_one, weight_dilated, bias_branch, weight_pool,
    bias_pool, weight_project, bias_project, weight_reduce, bias_reduce, weight_merging,
    bias_merging,
):
    mb, rows, cols, ch = features.shape
    br_w = weight_project.shape[1]
    low_w, lowp = weight_reduce.shape
    nb, ns = lax.axis_size("band"), lax.axis_size("sect")
    nx = ns // 2
    cs = cols // nx
    assert mb == 2 and ns % 2 == 0
    live = rows // LAND_BLOCK * LAND_MOST if rows % LAND_BLOCK == 0 else rows
    off, order = plan(rows, nb)
    n_off = max(len(off), 1)
    n_all = len(off) + 4
    pad = -(-max(DILATIONS) // 8) * 8
    vm, dma = pltpu.VMEM, pltpu.SemaphoreType.DMA
    dims = (mb, rows, cols, ch, br_w, live, nb, ns, low_w, lowp)
    scratch = [
        vm(features.shape, BF16),
        vm(low_level.shape, BF16),
        vm((2, mb, cols, low_w), BF16),
        vm(weight_one.shape, BF16),
        vm((3 + len(off), 3, ch, br_w), BF16),
        vm(weight_pool.shape, BF16),
        vm(weight_project.shape, BF16),
        vm((3, 3 * br_w, weight_merging.shape[3]), BF16),
        vm((3, 3, lowp, weight_merging.shape[3]), BF16),
        vm((mb, live, cols, ch), BF16),
        vm((rows, cols + 2 * pad, br_w), F32),
        vm((rows, cols + 2 * pad, br_w), F32),
        vm((n_off, 2, rows, cols, br_w), BF16),
        vm((n_off, rows, cols, br_w), BF16),
        vm((n_off, nx, live, cs, br_w), BF16),
        vm((n_off, nx, live, cs, br_w), BF16),
        vm((n_off, live, cs, br_w), BF16),
        vm((n_off, live, cs, br_w), BF16),
        vm((4, 2, live, cols, br_w), BF16),
        vm((4, live, cols, br_w), BF16),
        vm((4, nx, live, cs, br_w), BF16),
        vm((4, nx, live, cs, br_w), BF16),
        vm((n_off, live, cs, br_w), F32),
        vm((4, live, cs, br_w), F32),
        vm((live, rows, br_w), F32),
        vm((n_off, live, rows, br_w), F32),
        vm((8, ch), F32),
        vm((ns, 8, br_w), F32),
        vm((nb, 8, br_w), F32),
        vm((nx, live, cs, br_w), BF16),
        vm((nx, live, cs, br_w), BF16),
        vm((2, ns, cs, br_w), BF16),
        vm((mb, rows + 2, cols, br_w), BF16),
        vm((mb, rows + 2, cols, lowp), BF16),
        vm((mb, live, cols, br_w), F32),
        vm((live, cols, br_w), F32),
        dma((19 + len(off),)),
        dma((n_off,)),
        dma((n_off,)),
        dma((2,)),
        dma((2,)),
        dma((n_all,)),
        dma((n_all,)),
        dma((n_all, nx)),
        dma((n_all, nx)),
        dma((n_off,)),
        dma((n_off,)),
        dma((ns,)),
        dma((ns,)),
        dma((nb,)),
        dma((nb,)),
        dma((nx,)),
        dma((nx,)),
        dma((nx,)),
        dma((nx,)),
        dma((2, nx)),
        dma((2, nx)),
        dma((2, nx)),
        dma((2, nx)),
    ]
    anym = pl.BlockSpec(memory_space=pl.ANY)
    vmem = pl.BlockSpec(memory_space=pltpu.VMEM)
    smem = pl.BlockSpec(memory_space=pltpu.SMEM)
    merged_map = pl.pallas_call(
        functools.partial(kernel, dims),
        out_shape=jax.ShapeDtypeStruct((mb, rows, cols, weight_merging.shape[3]), BF16),
        in_specs=[
            smem, anym, anym, anym, anym, vmem, anym, vmem, anym, vmem, vmem, vmem, anym, vmem,
        ],
        out_specs=vmem,
        scratch_shapes=scratch,
        compiler_params=pltpu.CompilerParams(
            collective_id=0, has_side_effects=True, vmem_limit_bytes=60 * 1024 * 1024
        ),
    )(
        land_mask, features, low_level, weight_one, weight_dilated, bias_branch, weight_pool,
        bias_pool.reshape(1, -1), weight_project, bias_project.reshape(1, -1), weight_reduce.T,
        bias_reduce.reshape(1, -1), weight_merging, bias_merging.reshape(1, -1),
    )
    return jnp.where(land_mask[:, :, None, None] != 0, merged_map, jnp.zeros_like(merged_map))


def solution(mesh):
    in_specs = (
        P("grp", "band", None, "sect"),
        P("grp", "band", None, None),
        P("grp", "band"),
        P("sect", None),
        P(None, None, None, "sect", None),
        P(),
        P("sect", None),
        P(),
        P(),
        P(),
        P(),
        P(),
        P(),
        P(),
    )
    out_specs = P("grp", "band", None, None)
    return jax.shard_map(shards, mesh=mesh, in_specs=in_specs, out_specs=out_specs, check_vma=False)
```
